32 devices in a mesh: groups: 2 (over x), tile: 16 (over z, y, core).
Axes of the slice: x: 2, y: 2, z: 4, core: 2. Of those that a mesh axis runs over, the one named last changes fastest.
Arguments:
- features: bfloat16 [2, 192, 160, 256], P('groups', 'tile'), parts along dimension 0, may hold values from -6 to 6
- cotangent: bfloat16 [2, 192, 160, 256], P('groups', 'tile'), parts along dimension 0, may hold values from -6 to 6
- weight_one: bfloat16 [256, 9, 256], replicated, may hold values from -0.125 to 0.125
- weight_two: bfloat16 [256, 9, 256], replicated, may hold values from -0.125 to 0.125
Outputs:
- block_out: bfloat16 [2, 192, 160, 256], P('groups', 'tile'), parts along dimension 0
- input_grad: bfloat16 [2, 192, 160, 256], P('groups', 'tile'), parts along dimension 0
- grad_one: float32 [256, 18, 256], P('tile', 'groups'), parts along dimension 1
- grad_two: float32 [256, 18, 256], P('tile', 'groups'), parts along dimension 1
The draws below stay inside these ranges and needn't reach their ends.
There are 2 independent parts, one for each index of `groups`. The reference program is written for one: setup_inputs(seed, part) draws one part's arguments, and reference() takes and returns one part's arrays. A program takes and returns all parts, laid end to end along the dimension named above; an argument that names none is the same for every part. Nothing has to cross between parts.
All inputs are finite; a program needn't handle non-finite values.
Results may differ from the reference program's by a relative error of at most 0.0032.
Values may be sent and summed in bfloat16 or wider, within the bound.
No kernel may reach another device: no remote copies, remote signals or barrier semaphores. Data moves between devices by JAX's collectives and lax.ppermute only.
A program may use at most 128 MiB of HBM per device.

```python
import jax
import jax.numpy as jnp

C = 256
MB = 1
W = 160
NH = 192


def spiked(drawn, key, source, target, shards_of, factor):
    def block_of(axis_at):
        return (jnp.arange(drawn.shape[axis_at]) // (drawn.shape[axis_at] // shards_of)).reshape((-1,) + (1,) * (drawn.ndim - 1 - axis_at))

    near = jax.random.permutation(key, shards_of)[block_of(target)]
    other_side = (block_of(target) + shards_of // 2) % shards_of
    return jnp.where((block_of(source) == near) | (block_of(source) == other_side), factor * drawn, drawn)


def levels(own_key, shape, split, low, high):
    factor_of, own = 1.0, jax.random.fold_in(own_key, 6)
    for position, shards_of in split:
        steps = jnp.exp(jax.random.uniform(jax.random.fold_in(own, position), (shards_of,), jnp.float32, low / len(split), high / len(split)))
        factor_of = factor_of * jnp.repeat(steps, shape[position] // shards_of).reshape([-1 if axis == position else 1 for axis in range(len(shape))])
    return factor_of


def bell_draw(stream_key, dims, width, most, pieces=(), kind=jnp.bfloat16):
    values = width * jax.random.normal(stream_key, dims, jnp.float32)
    if pieces:
        values = values * levels(stream_key, dims, pieces, -0.22, 0.18)
    return jnp.clip(values, -most, most).astype(kind)


def gaussian_with(key, shape, scale, bound, split, heavy, dtype=jnp.bfloat16):
    drawn = scale * jax.random.normal(key, shape, jnp.float32)
    if split:
        drawn = drawn * levels(key, shape, split, -0.22, 0.18)
    return jnp.clip(spiked(drawn, jax.random.fold_in(key, 3), *heavy), -bound, bound).astype(dtype)


def setup_inputs(seed: int = 0, part: int = 0) -> dict:
    keys = jax.random.split(jax.random.key(seed), 5)
    own_keys = jax.random.split(jax.random.fold_in(keys[4], part), 5)
    features = gaussian_with(own_keys[0], (MB, NH, W, C), 1.0, 6.0, ((1, 16),), (1, 3, 16, 2.0))
    cotangent = bell_draw(own_keys[1], (MB, NH, W, C), 1.0, 6.0, ((1, 16),))
    weight_one = bell_draw(keys[2], (C, 9, C), (9 * C) ** -0.5, 0.125)
    weight_two = bell_draw(keys[3], (C, 9, C), (9 * C) ** -0.5, 0.125)
    return {"features": features, "cotangent": cotangent, "weight_one": weight_one, "weight_two": weight_two}


def pad_field(field):
    return jnp.pad(field.astype(jnp.float32), ((0, 0), (1, 1), (1, 1), (0, 0)))

def window(padded, tap_index, row_count, col_count, direction):
    row_shift = direction * (tap_index // 3 - 1)
    col_shift = direction * (tap_index % 3 - 1)
    return padded[:, 1 + row_shift:1 + row_shift + row_count, 1 + col_shift:1 + col_shift + col_count, :]

def conv_forward(field, kernel):
    padded = pad_field(field)
    kernel_f = kernel.astype(jnp.float32)
    total = jnp.zeros(field.shape, jnp.float32)
    for tap_index in range(9):
        piece = window(padded, tap_index, field.shape[1], field.shape[2], 1)
        total = total + jnp.einsum('brwi,io->brwo', piece, kernel_f[:, tap_index, :])
    return total

def conv_transpose(field, kernel):
    padded = pad_field(field)
    kernel_f = kernel.astype(jnp.float32)
    total = jnp.zeros(field.shape, jnp.float32)
    for tap_index in range(9):
        piece = window(padded, tap_index, field.shape[1], field.shape[2], -1)
        total = total + jnp.einsum('brwo,io->brwi', piece, kernel_f[:, tap_index, :])
    return total

def kernel_grad(source, grad):
    padded = pad_field(source)
    grad_f = grad.astype(jnp.float32)
    taps = []
    for tap_index in range(9):
        piece = window(padded, tap_index, source.shape[1], source.shape[2], 1)
        taps.append(jnp.einsum('brwi,brwo->io', piece, grad_f))
    return jnp.stack(taps, axis=1)

def reference(features, cotangent, weight_one, weight_two):
    scale = float(MB * NH * W) ** (-0.5)
    pre = conv_forward(features, weight_one)
    hidden = jax.nn.silu(pre).astype(jnp.bfloat16)
    block_out = (features.astype(jnp.float32) + conv_forward(hidden, weight_two)).astype(jnp.bfloat16)
    hidden_grad = conv_transpose(cotangent, weight_two)
    sigma = jax.nn.sigmoid(pre)
    slope = (hidden_grad * sigma * (1.0 + pre * (1.0 - sigma))).astype(jnp.bfloat16)
    input_grad = (cotangent.astype(jnp.float32) + conv_transpose(slope, weight_one)).astype(jnp.bfloat16)
    grad_one = kernel_grad(features, slope) * scale
    grad_two = kernel_grad(hidden, cotangent) * scale
    return (block_out, input_grad, grad_one, grad_two)
```

```python
import functools

import jax
import jax.numpy as jnp
from jax import lax
from jax.experimental import pallas as pl
from jax.experimental.pallas import tpu as pltpu
from jax.sharding import PartitionSpec as P

F32 = jnp.float32
BF16 = jnp.bfloat16
WHOLE = pl.BlockSpec(memory_space=pltpu.VMEM)
LIMIT = 40 << 20


def run(kernel, outs, args, scratch=(), flops=0):
    nbytes = sum(a.size * a.dtype.itemsize for a in list(args) + list(outs))
    return pl.pallas_call(
        kernel,
        out_shape=outs,
        in_specs=[WHOLE] * len(args),
        out_specs=tuple(WHOLE for _ in outs),
        scratch_shapes=list(scratch),
        compiler_params=pltpu.CompilerParams(vmem_limit_bytes=LIMIT),
        cost_estimate=pl.CostEstimate(flops=flops, bytes_accessed=nbytes, transcendentals=0),
    )(*args)


def struct(shape, dtype):
    return jax.ShapeDtypeStruct(shape, dtype)


def pack_kernel(f_first, c_first, f_last, c_last, first, last):
    first[0:2] = f_first[...]
    first[2:4] = c_first[...]
    last[0:2] = f_last[...]
    last[2:4] = c_last[...]


def pack(features, cotangent):
    rows, cols, chans = features.shape
    block = (2, cols, chans)
    end = rows // 2 - 1
    first = pl.BlockSpec(block, lambda i: (0, 0, 0))
    last = pl.BlockSpec(block, lambda i: (end, 0, 0))
    out = struct((4, cols, chans), BF16)
    whole = pl.BlockSpec((4, cols, chans), lambda i: (0, 0, 0))
    return pl.pallas_call(
        pack_kernel,
        grid=(1,),
        out_shape=(out, out),
        in_specs=[first, first, last, last],
        out_specs=(whole, whole),
        compiler_params=pltpu.CompilerParams(vmem_limit_bytes=8 << 20),
    )(features, cotangent, features, cotangent)


def put_windows(dst, row, value, sign):
    cols, chans = value.shape
    wide = value.astype(F32)
    index = lax.broadcasted_iota(jnp.int32, (cols, chans), 0)
    before = jnp.where(index == 0, 0.0, pltpu.roll(wide, 1, 0)).astype(BF16)
    after = jnp.where(index == cols - 1, 0.0, pltpu.roll(wide, cols - 1, 0)).astype(BF16)
    here = pl.ds(pl.multiple_of(row * cols, cols), cols)
    low, high = (before, after) if sign > 0 else (after, before)
    dst[here, 0:chans] = low
    dst[here, chans : 2 * chans] = value
    dst[here, 2 * chans : 3 * chans] = high


def fill(dst, base, count, source, first, sign):
    def step(k, carry):
        put_windows(dst, base + k, source[first + k], sign)
        return carry

    lax.fori_loop(0, count, step, 0)


def conv_rows(win, weight, start, size, cols):
    left = jnp.concatenate(
        [win[pl.ds(pl.multiple_of(start + a * cols, cols), size), :] for a in range(3)], axis=1
    )
    return jnp.dot(left, weight[...], preferred_element_type=F32)


def conv_t_rows(win, weight, start, size, cols, chans):
    total = None
    for a in range(3):
        left = win[pl.ds(pl.multiple_of(start + (2 - a) * cols, cols), size), :]
        for b in range(3):
            tap = (a * 3 + b) * chans
            part = lax.dot_general(
                left[:, b * chans : (b + 1) * chans],
                weight[tap : tap + chans, :],
                (((1,), (1,)), ((), ())),
                preferred_element_type=F32,
            )
            total = part if total is None else total + part
    return total


def bit_order(count, order):
    bits = [b for b in order[1:]]
    return bits


def slot_static(j, bits):
    s = 0
    for b in bits:
        s = s * 2 + ((j >> b) & 1)
    return s


def slot_dynamic(me, bits):
    s = jnp.int32(0)
    for b in bits:
        s = s * 2 + ((me >> b) & 1)
    return s


def store_terms(tap, value, keep, send, me, n, order, scale):
    rows = value.shape[0] // n
    value = value * scale
    bits = bit_order(n, order)
    mine = slot_dynamic(me, bits)
    flip = ((me >> order[0]) & 1) == 1
    for j in range(n):
        if (j >> order[0]) & 1:
            continue
        other = j ^ (1 << order[0])
        low = value[j * rows : (j + 1) * rows]
        high = value[other * rows : (other + 1) * rows]
        slot = slot_static(j, bits) ^ mine
        keep[slot, tap] = jnp.where(flip, high, low)
        send[slot, tap] = jnp.where(flip, low, high).astype(BF16)


def kernel_terms(left, win, keep, send, me, n, order, scale, cols, size):
    chans = left.shape[1]
    for a in range(3):
        right = win[(2 - a) * cols : (2 - a) * cols + size, :]
        out = lax.dot_general(left, right, (((0,), (0,)), ((), ())), preferred_element_type=F32)
        for b in range(3):
            store_terms(
                a * 3 + b, out[:, b * chans : (b + 1) * chans], keep, send, me, n, order, scale
            )


def forward_kernel(n, order, scale, me_ref, f, up, down, c, w, hid, fac, keep, send, xs, cs):
    rows, cols, chans = f.shape
    me = me_ref[0]
    fill(xs, 0, 2, up, 0, 1)
    fill(xs, 2, rows, f, 0, 1)
    fill(xs, rows + 2, 2, down, 0, 1)
    fill(cs, 0, 1, up, 3, -1)
    fill(cs, 1, rows, c, 0, -1)
    fill(cs, rows + 1, 1, down, 2, -1)
    half = (rows + 2) // 2
    size = half * cols

    def step(k, carry):
        start = k * size
        pre = conv_rows(xs, w, start, size, cols)
        sigma = jax.nn.sigmoid(pre)
        here = pl.ds(pl.multiple_of(start, cols), size)
        hid[here, :] = (pre * sigma).astype(BF16)
        fac[here, :] = sigma * (1.0 + pre * (1.0 - sigma))
        return carry

    lax.fori_loop(0, 2, step, 0)

    @pl.when(me == 0)
    def _():
        hid[0:cols, :] = jnp.zeros((cols, chans), BF16)
        fac[0:cols, :] = jnp.zeros((cols, chans), F32)

    @pl.when(me == n - 1)
    def _():
        hid[(rows + 1) * cols : (rows + 2) * cols, :] = jnp.zeros((cols, chans), BF16)
        fac[(rows + 1) * cols : (rows + 2) * cols, :] = jnp.zeros((cols, chans), F32)

    own = hid[cols : (rows + 1) * cols, :]
    kernel_terms(own, cs, keep, send, me, n, order, scale, cols, rows * cols)


def slope_kernel(n, order, scale, me_ref, c, up, down, f, fac, w, slope, keep, send, cs, ss):
    rows, cols, chans = c.shape
    me = me_ref[0]
    fill(cs, 0, 2, up, 2, -1)
    fill(cs, 2, rows, c, 0, -1)
    fill(cs, rows + 2, 2, down, 2, -1)
    half = (rows + 2) // 2
    size = half * cols

    def step(k, carry):
        start = k * size
        grad = conv_t_rows(cs, w, start, size, cols, chans)
        here = pl.ds(pl.multiple_of(start, cols), size)
        slope[here, :] = (grad * fac[here, :]).astype(BF16)
        return carry

    lax.fori_loop(0, 2, step, 0)

    def widen(k, carry):
        here = pl.ds(pl.multiple_of(k * cols, cols), cols)
        put_windows(ss, k, slope[here, :], -1)
        return carry

    lax.fori_loop(0, rows + 2, widen, 0)
    own = f[...].reshape(rows * cols, chans)
    kernel_terms(own, ss, keep, send, me, n, order, scale, cols, rows * cols)


def outputs_kernel(hid, slope, f, c, w_one, w_two, block_out, input_grad, hs, ss):
    rows, cols, chans = f.shape

    def widen(k, carry):
        here = pl.ds(pl.multiple_of(k * cols, cols), cols)
        put_windows(hs, k, hid[here, :], 1)
        put_windows(ss, k, slope[here, :], -1)
        return carry

    lax.fori_loop(0, rows + 2, widen, 0)
    half = rows // 2
    size = half * cols

    def step(k, carry):
        start = k * size
        here = pl.ds(k * half, half)
        out = conv_rows(hs, w_two, start, size, cols)
        block_out[here] = (f[here].astype(F32) + out.reshape(half, cols, chans)).astype(BF16)
        out = conv_t_rows(ss, w_one, start, size, cols, chans)
        input_grad[here] = (c[here].astype(F32) + out.reshape(half, cols, chans)).astype(BF16)
        return carry

    lax.fori_loop(0, 2, step, 0)


def halve(keep, send, order, n):
    for stage, bit in enumerate(order):
        pairs = [(i, i ^ (1 << bit)) for i in range(n)]
        got = lax.ppermute(send, "tile", pairs)
        total = keep + got.astype(F32)
        half = total.shape[0] // 2
        if half:
            keep, send = total[:half], total[half:].astype(BF16)
        else:
            return jnp.swapaxes(total[0], 0, 1)


def body(features, cotangent, weight_one, weight_two):
    _, rows, cols, chans = features.shape
    n = lax.axis_size("tile")
    scale = float(rows * n * cols) ** (-0.5)
    me = lax.axis_index("tile").astype(jnp.int32).reshape(1)
    f, c = features[0], cotangent[0]
    taps = weight_one.shape[1]
    w_one = jnp.swapaxes(weight_one, 0, 1).reshape(taps * chans, chans)
    w_two = jnp.swapaxes(weight_two, 0, 1).reshape(taps * chans, chans)

    first, last = pack(f, c)
    up = lax.ppermute(last, "tile", [(i, i + 1) for i in range(n - 1)])
    down = lax.ppermute(first, "tile", [(i + 1, i) for i in range(n - 1)])

    bits = n.bit_length() - 1
    order_two = list(range(bits))
    order_one = [0, 2, 1] + list(range(3, bits)) if bits > 2 else order_two
    block = chans // n
    term = (n // 2, taps, block, chans)
    ext = (rows + 2) * cols
    flops = 2 * 9 * rows * cols * chans * chans
    smem = pl.BlockSpec(memory_space=pltpu.SMEM)

    def call(kernel, args, outs, scratch, work):
        return pl.pallas_call(
            kernel,
            out_shape=outs,
            in_specs=[smem] + [WHOLE] * len(args),
            out_specs=tuple(WHOLE for _ in outs),
            scratch_shapes=scratch,
            compiler_params=pltpu.CompilerParams(vmem_limit_bytes=LIMIT),
            cost_estimate=pl.CostEstimate(flops=work, bytes_accessed=8 << 20, transcendentals=0),
        )(me, *args)

    wide = 3 * chans
    hid, fac, keep_two, send_two = call(
        functools.partial(forward_kernel, n, order_two, scale),
        (f, up, down, c, w_one),
        (struct((ext, chans), BF16), struct((ext, chans), F32), struct(term, F32), struct(term, BF16)),
        [pltpu.VMEM(((rows + 4) * cols, wide), BF16), pltpu.VMEM((ext, wide), BF16)],
        2 * flops,
    )
    slope, keep_one, send_one = call(
        functools.partial(slope_kernel, n, order_one, scale),
        (c, up, down, f, fac, w_two),
        (struct((ext, chans), BF16), struct(term, F32), struct(term, BF16)),
        [pltpu.VMEM(((rows + 4) * cols, wide), BF16), pltpu.VMEM((ext, wide), BF16)],
        2 * flops,
    )
    block_out, input_grad = run(
        outputs_kernel,
        (struct(f.shape, BF16), struct(f.shape, BF16)),
        (hid, slope, f, c, w_one, w_two),
        [pltpu.VMEM((ext, wide), BF16), pltpu.VMEM((ext, wide), BF16)],
        2 * flops,
    )
    grad_two = halve(keep_two, send_two, order_two, n)
    grad_one = halve(keep_one, send_one, order_one, n)
    return (block_out[None], input_grad[None], grad_one, grad_two)


def solution(mesh):
    in_specs = (P("groups", "tile", None, None), P("groups", "tile", None, None), P(), P())
    out_specs = (
        P("groups", "tile", None, None),
        P("groups", "tile", None, None),
        P("tile", "groups", None),
        P("tile", "groups", None),
    )
    return jax.shard_map(body, mesh=mesh, in_specs=in_specs, out_specs=out_specs, check_vma=False)
```

```python
import functools

import jax
import jax.numpy as jnp
from jax import lax
from jax.experimental import pallas as pl
from jax.experimental.pallas import tpu as pltpu
from jax.sharding import PartitionSpec as P


F32 = jnp.float32
BF16 = jnp.bfloat16
WHOLE = pl.BlockSpec(memory_space=pltpu.VMEM)
LIMIT = 20 << 20


def struct(shape, dtype):
    return jax.ShapeDtypeStruct(shape, dtype)


def pack_kernel(f, c, first, last, second, before_last, sems):
    rows = f.shape[0]
    copies = []
    for out, row in ((first, 0), (last, rows - 1), (second, 1), (before_last, rows - 2)):
        for k, field in enumerate((f, c)):
            copies.append(pltpu.make_async_copy(field.at[row], out.at[k], sems.at[len(copies)]))
    for copy in copies:
        copy.start()
    for copy in copies:
        copy.wait()


def pack(features, cotangent):
    out = struct((2,) + features.shape[1:], BF16)
    hbm = pl.BlockSpec(memory_space=pltpu.HBM)
    return pl.pallas_call(
        pack_kernel,
        out_shape=(out,) * 4,
        in_specs=[hbm, hbm],
        out_specs=(WHOLE,) * 4,
        scratch_shapes=[pltpu.SemaphoreType.DMA((8,))],
        compiler_params=pltpu.CompilerParams(vmem_limit_bytes=8 << 20),
    )(
        pltpu.with_memory_space_constraint(features, pltpu.HBM),
        pltpu.with_memory_space_constraint(cotangent, pltpu.HBM),
    )


def put_windows(dst, row, value, sign):
    cols, chans = value.shape
    wide = value.astype(F32)
    index = lax.broadcasted_iota(jnp.int32, (cols, chans), 0)
    before = jnp.where(index == 0, 0.0, pltpu.roll(wide, 1, 0)).astype(BF16)
    after = jnp.where(index == cols - 1, 0.0, pltpu.roll(wide, cols - 1, 0)).astype(BF16)
    here = pl.ds(pl.multiple_of(row * cols, cols), cols)
    low, high = (before, after) if sign > 0 else (after, before)
    dst[here, 0:chans] = low
    dst[here, chans : 2 * chans] = value
    dst[here, 2 * chans : 3 * chans] = high


def fill(dst, base, count, source, first, sign):
    def step(k, carry):
        put_windows(dst, base + k, source[first + k], sign)
        return carry

    lax.fori_loop(0, count, step, 0)


def conv_rows(win, weight, start, size, cols):
    left = jnp.concatenate(
        [win[pl.ds(pl.multiple_of(start + a * cols, cols), size), :] for a in range(3)], axis=1
    )
    return jnp.dot(left, weight[...], preferred_element_type=F32)


def conv_t_rows(win, weight, start, size, cols, chans):
    total = None
    for a in range(3):
        left = win[pl.ds(pl.multiple_of(start + (2 - a) * cols, cols), size), :]
        for b in range(3):
            tap = (a * 3 + b) * chans
            part = lax.dot_general(
                left[:, b * chans : (b + 1) * chans],
                weight[tap : tap + chans, :],
                (((1,), (1,)), ((), ())),
                preferred_element_type=F32,
            )
            total = part if total is None else total + part
    return total


def bit_order(order):
    bits = [b for b in order[1:]]
    return bits


def slot_static(j, bits):
    s = 0
    for b in bits:
        s = s * 2 + ((j >> b) & 1)
    return s


def slot_dynamic(me, bits):
    s = jnp.int32(0)
    for b in bits:
        s = s * 2 + ((me >> b) & 1)
    return s


def store_terms(tap, value, keep, send, me, n, order, scale):
    rows = value.shape[0] // n
    value = value * scale
    bits = bit_order(order)
    mine = slot_dynamic(me, bits)
    flip = ((me >> order[0]) & 1) == 1
    for j in range(n):
        if (j >> order[0]) & 1:
            continue
        other = j ^ (1 << order[0])
        low = value[j * rows : (j + 1) * rows]
        high = value[other * rows : (other + 1) * rows]
        slot = slot_static(j, bits) ^ mine
        keep[slot, tap] = jnp.where(flip, high, low)
        send[slot, tap] = jnp.where(flip, low, high).astype(BF16)


def kernel_terms(left, win, keep, send, me, n, order, scale, cols, size):
    chans = left.shape[1]
    for a in range(3):
        right = win[(2 - a) * cols : (2 - a) * cols + size, :]
        out = lax.dot_general(left, right, (((0,), (0,)), ((), ())), preferred_element_type=F32)
        for b in range(3):
            store_terms(
                a * 3 + b, out[:, b * chans : (b + 1) * chans], keep, send, me, n, order, scale
            )


def activation(pre, hid, fac, here):
    sigma = jax.nn.sigmoid(pre)
    hid[here, :] = (pre * sigma).astype(BF16)
    fac[here, :] = sigma * (1.0 + pre * (1.0 - sigma))


def inner_kernel(f, c, w, xs, cs, hid, fac):
    rows, cols, _ = f.shape
    fill(xs, 1, rows, f, 0, 1)
    half = (rows - 2) // 2
    size = half * cols

    def step(k, carry):
        start = (1 + k * half) * cols
        pre = conv_rows(xs, w, start, size, cols)
        activation(pre, hid, fac, pl.ds(pl.multiple_of(start, cols), size))
        return carry

    lax.fori_loop(0, 2, step, 0)
    fill(cs, 1, rows, c, 0, -1)


def edge_kernel(n, order, scale, me_ref, up, down, w, xs_in, cs_in, hid_in, fac_in,
                xs, cs, hid, fac, keep, send):
    cols, _ = up.shape[1:]
    rows = xs.shape[0] // cols - 2
    put_windows(xs, 0, up[0], 1)
    put_windows(xs, rows + 1, down[0], 1)
    put_windows(cs, 0, up[1], -1)
    put_windows(cs, rows + 1, down[1], -1)
    left = jnp.concatenate(
        [
            jnp.concatenate(
                [xs[a * cols : (a + 1) * cols, :], xs[(rows - 1 + a) * cols : (rows + a) * cols, :]],
                axis=0,
            )
            for a in range(3)
        ],
        axis=1,
    )
    pre = jnp.dot(left, w[...], preferred_element_type=F32)
    activation(pre[:cols], hid, fac, pl.ds(0, cols))
    activation(pre[cols:], hid, fac, pl.ds((rows - 1) * cols, cols))
    kernel_terms(hid[...], cs, keep, send, me_ref[0], n, order, scale, cols, rows * cols)


def slope_kernel(cs, fac, w, slope):
    size_all, chans = slope.shape
    cols = (cs.shape[0] - size_all) // 2
    rows = size_all // cols
    half = rows // 2
    size = half * cols

    def step(k, carry):
        start = k * size
        grad = conv_t_rows(cs, w, start, size, cols, chans)
        here = pl.ds(pl.multiple_of(start, cols), size)
        slope[here, :] = (grad * fac[here, :]).astype(BF16)
        return carry

    lax.fori_loop(0, 2, step, 0)


def terms_kernel(n, order, scale, me_ref, xs, slope, keep, send):
    size_all, chans = slope.shape
    cols = (xs.shape[0] - size_all) // 2
    for a in range(3):
        left = xs[a * cols : a * cols + size_all, :]
        out = lax.dot_general(left, slope[...], (((0,), (0,)), ((), ())), preferred_element_type=F32)
        for b in range(3):
            store_terms(
                a * 3 + b, out[b * chans : (b + 1) * chans], keep, send, me_ref[0], n, order, scale
            )


def row_of(ref, k, cols):
    return ref[k * cols : (k + 1) * cols, :]


def edges_kernel(n, me_ref, xs, cs, up, down, w_one, w_two, hid_edge, slope_edge, xe, ce):
    cols, chans = up.shape[1:]
    rows = xs.shape[0] // cols - 2
    put_windows(xe, 0, up[0], 1)
    put_windows(xe, 1, down[0], 1)
    put_windows(ce, 0, up[1], -1)
    put_windows(ce, 1, down[1], -1)

    def pair(one, j, two, k):
        return jnp.concatenate([row_of(one, j, cols), row_of(two, k, cols)], axis=0)

    left = jnp.concatenate(
        [pair(xe, 0, xs, rows), pair(xs, 0, xs, rows + 1), pair(xs, 1, xe, 1)], axis=1
    )
    pre = jnp.dot(left, w_one[...], preferred_element_type=F32)
    total = None
    for a, left in enumerate((pair(cs, 1, ce, 1), pair(cs, 0, cs, rows + 1), pair(ce, 0, cs, rows))):
        for b in range(3):
            tap = (a * 3 + b) * chans
            part = lax.dot_general(
                left[:, b * chans : (b + 1) * chans],
                w_two[tap : tap + chans, :],
                (((1,), (1,)), ((), ())),
                preferred_element_type=F32,
            )
            total = part if total is None else total + part
    sigma = jax.nn.sigmoid(pre)
    hidden = pre * sigma
    slope = total * sigma * (1.0 + pre * (1.0 - sigma))
    for side, outside in ((0, me_ref[0] == 0), (1, me_ref[0] == n - 1)):
        here = slice(side * cols, (side + 1) * cols)
        hid_edge[here, :] = jnp.where(outside, 0.0, hidden[here]).astype(BF16)
        slope_edge[here, :] = jnp.where(outside, 0.0, slope[here]).astype(BF16)


def widen(dst, edge, own, rows, cols, sign):
    put_windows(dst, 0, row_of(edge, 0, cols), sign)
    put_windows(dst, rows + 1, row_of(edge, 1, cols), sign)

    def step(k, carry):
        put_windows(dst, k + 1, own[pl.ds(pl.multiple_of(k * cols, cols), cols), :], sign)
        return carry

    lax.fori_loop(0, rows, step, 0)


def block_kernel(hid_edge, hid, w_two, f, block_out, hs):
    rows, cols, chans = f.shape
    widen(hs, hid_edge, hid, rows, cols, 1)
    half = rows // 2
    size = half * cols

    def step(k, carry):
        here = pl.ds(k * half, half)
        out = conv_rows(hs, w_two, k * size, size, cols)
        block_out[here] = (f[here].astype(F32) + out.reshape(half, cols, chans)).astype(BF16)
        return carry

    lax.fori_loop(0, 2, step, 0)


def input_kernel(slope_edge, slope, w_one, c, input_grad, ss):
    rows, cols, chans = c.shape
    widen(ss, slope_edge, slope, rows, cols, -1)
    half = rows // 2
    size = half * cols

    def step(k, carry):
        here = pl.ds(k * half, half)
        out = conv_t_rows(ss, w_one, k * size, size, cols, chans)
        input_grad[here] = (c[here].astype(F32) + out.reshape(half, cols, chans)).astype(BF16)
        return carry

    lax.fori_loop(0, 2, step, 0)


def halve(keep, send, order, n):
    for bit in order:
        pairs = [(i, i ^ (1 << bit)) for i in range(n)]
        got = lax.ppermute(send, "tile", pairs)
        total = keep + got.astype(F32)
        half = total.shape[0] // 2
        if half:
            keep, send = total[:half], total[half:].astype(BF16)
        else:
            return jnp.swapaxes(total[0], 0, 1)


def layer(features, cotangent, weight_one, weight_two):
    _, rows, cols, chans = features.shape
    n = lax.axis_size("tile")
    scale = float(rows * n * cols) ** (-0.5)
    me = lax.axis_index("tile").astype(jnp.int32).reshape(1)
    f, c = features[0], cotangent[0]
    taps = weight_one.shape[1]
    w_one = jnp.swapaxes(weight_one, 0, 1).reshape(taps * chans, chans)
    w_two = jnp.swapaxes(weight_two, 0, 1).reshape(taps * chans, chans)

    bits = n.bit_length() - 1
    order_two = list(range(bits))
    order_one = [0, 2, 1] + list(range(3, bits)) if bits > 2 else order_two
    size, ext, wide = rows * cols, (rows + 2) * cols, 3 * chans
    flops = 2 * 9 * size * chans * chans
    smem = pl.BlockSpec(memory_space=pltpu.SMEM)

    def call(kernel, args, outs, scratch=(), work=flops, place=False, aliases={}):
        return pl.pallas_call(
            kernel,
            out_shape=outs,
            in_specs=([smem] if place else []) + [WHOLE] * len(args),
            out_specs=tuple(WHOLE for _ in outs),
            scratch_shapes=list(scratch),
            input_output_aliases=aliases,
            compiler_params=pltpu.CompilerParams(vmem_limit_bytes=LIMIT),
            cost_estimate=pl.CostEstimate(flops=work, bytes_accessed=4 << 20, transcendentals=0),
        )(*(((me,) if place else ()) + tuple(args)))

    upward = [(i, i + 1) for i in range(n - 1)]
    downward = [(i + 1, i) for i in range(n - 1)]
    first, last, second, before_last = pack(f, c)
    up = lax.ppermute(last, "tile", upward)
    down = lax.ppermute(first, "tile", downward)

    windows = struct((ext, wide), BF16)
    field, field_wide = struct((size, chans), BF16), struct((size, chans), F32)
    kept = struct((n // 2, taps, chans // n, chans), F32)
    sent = struct((n // 2, taps, chans // n, chans), BF16)
    xs, cs, hid, fac = call(inner_kernel, (f, c, w_one), (windows, windows, field, field_wide))
    xs, cs, hid, fac, keep_two, send_two = call(
        functools.partial(edge_kernel, n, order_two, scale),
        (up, down, w_one, xs, cs, hid, fac),
        (windows, windows, field, field_wide, kept, sent),
        place=True,
        aliases={4: 0, 5: 1, 6: 2, 7: 3},
    )
    up_two = lax.ppermute(before_last, "tile", upward)
    down_two = lax.ppermute(second, "tile", downward)
    (slope,) = call(slope_kernel, (cs, fac, w_two), (field,))
    keep_one, send_one = call(
        functools.partial(terms_kernel, n, order_one, scale), (xs, slope), (kept, sent), place=True
    )
    edge_pair = struct((2 * cols, chans), BF16)
    edge_rows = pltpu.VMEM((2 * cols, wide), BF16)
    all_rows = pltpu.VMEM((ext, wide), BF16)
    hid_edge, slope_edge = call(
        functools.partial(edges_kernel, n),
        (xs, cs, up_two, down_two, w_one, w_two),
        (edge_pair, edge_pair),
        [edge_rows, edge_rows],
        place=True,
    )
    (block_out,) = call(
        block_kernel, (hid_edge, hid, w_two, f), (struct(f.shape, BF16),), [all_rows]
    )
    (input_grad,) = call(
        input_kernel, (slope_edge, slope, w_one, c), (struct(c.shape, BF16),), [all_rows]
    )
    grad_two = halve(keep_two, send_two, order_two, n)
    grad_one = halve(keep_one, send_one, order_one, n)
    return (block_out[None], input_grad[None], grad_one, grad_two)


def solution(mesh):
    in_specs = (P("groups", "tile", None, None), P("groups", "tile", None, None), P(), P())
    out_specs = (
        P("groups", "tile", None, None),
        P("groups", "tile", None, None),
        P("tile", "groups", None),
        P("tile", "groups", None),
    )
    return jax.shard_map(layer, mesh=mesh, in_specs=in_specs, out_specs=out_specs, check_vma=False)
```

```python
import functools

import jax
import jax.numpy as jnp
from jax import lax
from jax.experimental import pallas as pl
from jax.experimental.pallas import tpu as pltpu
from jax.sharding import PartitionSpec as P


F32 = jnp.float32
BF16 = jnp.bfloat16
WHOLE = pl.BlockSpec(memory_space=pltpu.VMEM)
LIMIT = 20 << 20


def struct(shape, dtype):
    return jax.ShapeDtypeStruct(shape, dtype)


def pack_kernel(me_ref, f, c, inside, across, sems):
    rows = f.shape[0]
    odd = (me_ref[0] & 1) == 1
    low, high = jnp.where(odd, 0, rows - 2), jnp.where(odd, rows - 2, 0)
    copies = []
    for out, row in ((across, high), (inside, low)):
        for k, field in enumerate((f, c)):
            copies.append(
                pltpu.make_async_copy(
                    field.at[pl.ds(row, 2)], out.at[pl.ds(2 * k, 2)], sems.at[len(copies)]
                )
            )
    for copy in copies:
        copy.start()
    for copy in copies:
        copy.wait()


def in_hbm(array):
    return pltpu.with_memory_space_constraint(array, pltpu.HBM)


def pack(me, features, cotangent):
    out = struct((4,) + features.shape[1:], BF16)
    hbm = pl.BlockSpec(memory_space=pltpu.HBM)
    return pl.pallas_call(
        pack_kernel,
        out_shape=(out,) * 2,
        in_specs=[pl.BlockSpec(memory_space=pltpu.SMEM), hbm, hbm],
        out_specs=(WHOLE,) * 2,
        scratch_shapes=[pltpu.SemaphoreType.DMA((4,))],
        compiler_params=pltpu.CompilerParams(vmem_limit_bytes=8 << 20),
    )(me, in_hbm(features), in_hbm(cotangent))


def put_windows(dst, row, value, sign):
    cols, chans = value.shape
    wide = value.astype(F32)
    index = lax.broadcasted_iota(jnp.int32, (cols, chans), 0)
    before = jnp.where(index == 0, 0.0, pltpu.roll(wide, 1, 0)).astype(BF16)
    after = jnp.where(index == cols - 1, 0.0, pltpu.roll(wide, cols - 1, 0)).astype(BF16)
    here = pl.ds(pl.multiple_of(row * cols, cols), cols)
    low, high = (before, after) if sign > 0 else (after, before)
    dst[here, 0:chans] = low
    dst[here, chans : 2 * chans] = value
    dst[here, 2 * chans : 3 * chans] = high


def fill(dst, base, count, source, first, sign):
    def step(k, carry):
        put_windows(dst, base + k, source[first + k], sign)
        return carry

    lax.fori_loop(0, count, step, 0)


def conv_rows(win, weight, start, size, cols):
    left = jnp.concatenate(
        [win[pl.ds(pl.multiple_of(start + a * cols, cols), size), :] for a in range(3)], axis=1
    )
    return jnp.dot(left, weight[...], preferred_element_type=F32)


def conv_t_rows(win, weight, start, size, cols, chans):
    total = None
    for a in range(3):
        left = win[pl.ds(pl.multiple_of(start + (2 - a) * cols, cols), size), :]
        for b in range(3):
            tap = (a * 3 + b) * chans
            part = lax.dot_general(
                left[:, b * chans : (b + 1) * chans],
                weight[tap : tap + chans, :],
                (((1,), (1,)), ((), ())),
                preferred_element_type=F32,
            )
            total = part if total is None else total + part
    return total


def bit_order(order):
    bits = [b for b in order[1:]]
    return bits


def slot_static(j, bits):
    s = 0
    for b in bits:
        s = s * 2 + ((j >> b) & 1)
    return s


def slot_dynamic(me, bits):
    s = jnp.int32(0)
    for b in bits:
        s = s * 2 + ((me >> b) & 1)
    return s


def store_terms(tap, value, keep, send, me, n, order, scale):
    rows = value.shape[0] // n
    value = value * scale
    bits = bit_order(order)
    mine = slot_dynamic(me, bits)
    flip = ((me >> order[0]) & 1) == 1
    for j in range(n):
        if (j >> order[0]) & 1:
            continue
        other = j ^ (1 << order[0])
        low = value[j * rows : (j + 1) * rows]
        high = value[other * rows : (other + 1) * rows]
        slot = slot_static(j, bits) ^ mine
        keep[slot, tap] = jnp.where(flip, high, low)
        send[slot, tap] = jnp.where(flip, low, high).astype(BF16)


def transposed_dot(left, right):
    return lax.dot_general(left, right, (((0,), (0,)), ((), ())), preferred_element_type=F32)


def rows_of(ref, first, count, cols):
    return ref[first * cols : (first + count) * cols, :]


def pair(ref, one, two, cols):
    return jnp.concatenate([rows_of(ref, one, 1, cols), rows_of(ref, two, 1, cols)], axis=0)


def pre_of_pair(xs, w, one, two, cols):
    left = [pair(xs, one + 1 + a, two + 1 + a, cols) for a in range(3)]
    return jnp.dot(jnp.concatenate(left, axis=1), w[...], preferred_element_type=F32)


def grad_of_pair(cs, w, one, two, cols):
    total = None
    for a in range(3):
        left = pair(cs, one + 3 - a, two + 3 - a, cols)
        chans = left.shape[1] // 3
        for b in range(3):
            tap = (a * 3 + b) * chans
            part = lax.dot_general(
                left[:, b * chans : (b + 1) * chans],
                w[tap : tap + chans, :],
                (((1,), (1,)), ((), ())),
                preferred_element_type=F32,
            )
            total = part if total is None else total + part
    return total


def derivative(pre, sigma):
    return sigma * (1.0 + pre * (1.0 - sigma))


def inner_kernel(f_hbm, c_hbm, w_hbm, w_one, xs, cs, hid, slope, acc, f, c, w_two, sems):
    rows, cols, chans = f.shape
    copy_f = pltpu.make_async_copy(f_hbm, f, sems.at[0])
    copy_c = pltpu.make_async_copy(c_hbm, c, sems.at[1])
    copy_w = pltpu.make_async_copy(w_hbm, w_two, sems.at[2])
    copy_f.start()
    copy_c.start()
    copy_w.start()
    copy_f.wait()
    fill(xs, 2, rows, f, 0, 1)
    copy_c.wait()
    fill(cs, 2, rows, c, 0, -1)
    copy_w.wait()
    half = (rows - 2) // 2
    size = half * cols

    def step(k, carry):
        start = (2 + k * half) * cols
        here = pl.ds(pl.multiple_of(start, cols), size)
        pre = conv_rows(xs, w_one, start, size, cols)
        sigma = jax.nn.sigmoid(pre)
        hid[here, :] = (pre * sigma).astype(BF16)
        grad = conv_t_rows(cs, w_two, start, size, cols, chans)
        slope[here, :] = (grad * derivative(pre, sigma)).astype(BF16)
        return carry

    lax.fori_loop(0, 2, step, 0)
    left = rows_of(hid, 2, rows - 2, cols)
    for a in range(3):
        acc[a] = transposed_dot(left, rows_of(cs, 4 - a, rows - 2, cols))


def edge_kernel(n, order, scale, me_ref, inside, across, w, xs_in, cs_in, hid_in, acc,
                xs, cs, hid, fac, keep, send):
    cols, chans = inside.shape[1:]
    rows = xs.shape[0] // cols - 4
    me = me_ref[0]
    odd = (me & 1) == 1
    for k in range(2):
        for dst, part, sign in ((xs, k, 1), (cs, 2 + k, -1)):
            one, two = inside[part], across[part]
            put_windows(dst, k, jnp.where(odd, one, two), sign)
            put_windows(dst, rows + 2 + k, jnp.where(odd, two, one), sign)
    pre = pre_of_pair(xs, w, 0, rows - 1, cols)
    sigma = jax.nn.sigmoid(pre)
    hidden = (pre * sigma).astype(BF16)
    hid[cols : 2 * cols, :] = hidden[:cols]
    hid[rows * cols : (rows + 1) * cols, :] = hidden[cols:]
    fac[...] = derivative(pre, sigma)
    left = pair(hid, 1, rows, cols)
    for a in range(3):
        out = acc[a] + transposed_dot(left, pair(cs, 3 - a, rows + 2 - a, cols))
        for b in range(3):
            store_terms(
                a * 3 + b, out[:, b * chans : (b + 1) * chans], keep, send, me, n, order, scale
            )


def terms_kernel(n, order, scale, me_ref, xs, cs, fac, w, slope_in, slope, keep, send):
    chans = slope.shape[1]
    cols = fac.shape[0] // 2
    rows = xs.shape[0] // cols - 4
    value = (grad_of_pair(cs, w, 0, rows - 1, cols) * fac[...]).astype(BF16)
    slope[cols : 2 * cols, :] = value[:cols]
    slope[rows * cols : (rows + 1) * cols, :] = value[cols:]
    right = rows_of(slope, 1, rows, cols)
    for a in range(3):
        out = transposed_dot(rows_of(xs, 1 + a, rows, cols), right)
        for b in range(3):
            store_terms(
                a * 3 + b, out[b * chans : (b + 1) * chans], keep, send, me_ref[0], n, order, scale
            )


def sides_kernel(n, cols, me_ref, xs, cs, w_one, w_two, hid_in, slope_in, hid, slope):
    rows = xs.shape[0] // cols - 4
    pre = pre_of_pair(xs, w_one, -1, rows, cols)
    grad = grad_of_pair(cs, w_two, -1, rows, cols)
    sigma = jax.nn.sigmoid(pre)
    hidden = pre * sigma
    value = grad * derivative(pre, sigma)
    for side, outside in ((0, me_ref[0] == 0), (1, me_ref[0] == n - 1)):
        here = slice(side * cols, (side + 1) * cols)
        there = slice(side * (rows + 1) * cols, (side * (rows + 1) + 1) * cols)
        hid[there, :] = jnp.where(outside, 0.0, hidden[here]).astype(BF16)
        slope[there, :] = jnp.where(outside, 0.0, value[here]).astype(BF16)


def widen(dst, source, count, cols, sign):
    def step(k, carry):
        put_windows(dst, k, source[pl.ds(pl.multiple_of(k * cols, cols), cols), :], sign)
        return carry

    lax.fori_loop(0, count, step, 0)


def block_kernel(hid, w_two, f, block_out, hs):
    rows, cols, chans = f.shape
    widen(hs, hid, rows + 2, cols, 1)
    half = rows // 2
    size = half * cols

    def step(k, carry):
        here = pl.ds(k * half, half)
        out = conv_rows(hs, w_two, k * size, size, cols)
        block_out[here] = (f[here].astype(F32) + out.reshape(half, cols, chans)).astype(BF16)
        return carry

    lax.fori_loop(0, 2, step, 0)


def input_kernel(slope, w_one, c, input_grad, ss):
    rows, cols, chans = c.shape
    widen(ss, slope, rows + 2, cols, -1)
    half = rows // 2
    size = half * cols

    def step(k, carry):
        here = pl.ds(k * half, half)
        out = conv_t_rows(ss, w_one, k * size, size, cols, chans)
        input_grad[here] = (c[here].astype(F32) + out.reshape(half, cols, chans)).astype(BF16)
        return carry

    lax.fori_loop(0, 2, step, 0)


def halve(keep, send, order, n):
    for bit in order:
        pairs = [(i, i ^ (1 << bit)) for i in range(n)]
        got = lax.ppermute(send, "tile", pairs)
        total = keep + got.astype(F32)
        half = total.shape[0] // 2
        if half:
            keep, send = total[:half], total[half:].astype(BF16)
        else:
            return jnp.swapaxes(total[0], 0, 1)


def layer(features, cotangent, weight_one, weight_two):
    _, rows, cols, chans = features.shape
    n = lax.axis_size("tile")
    scale = float(rows * n * cols) ** (-0.5)
    me = lax.axis_index("tile").astype(jnp.int32).reshape(1)
    f, c = features[0], cotangent[0]
    taps = weight_one.shape[1]
    w_one = jnp.swapaxes(weight_one, 0, 1).reshape(taps * chans, chans)
    w_two = jnp.swapaxes(weight_two, 0, 1).reshape(taps * chans, chans)

    bits = n.bit_length() - 1
    order_two = list(range(bits))
    order_one = [0, 2, 1] + list(range(3, bits)) if bits > 2 else order_two
    size, ext, wide = rows * cols, (rows + 2) * cols, 3 * chans
    flops = 2 * 9 * size * chans * chans
    smem = pl.BlockSpec(memory_space=pltpu.SMEM)

    hbm = pl.BlockSpec(memory_space=pltpu.HBM)

    def call(kernel, args, outs, scratch=(), work=flops, place=False, aliases={}, raw=0):
        specs = ([smem] if place else []) + [hbm] * raw + [WHOLE] * (len(args) - raw)
        return pl.pallas_call(
            kernel,
            out_shape=outs,
            in_specs=specs,
            out_specs=tuple(WHOLE for _ in outs),
            scratch_shapes=list(scratch),
            input_output_aliases=aliases,
            compiler_params=pltpu.CompilerParams(vmem_limit_bytes=LIMIT),
            cost_estimate=pl.CostEstimate(flops=work, bytes_accessed=4 << 20, transcendentals=0),
        )(*(((me,) if place else ()) + tuple(args)))

    inside, across = pack(me, f, c)
    pairs = [(i, i + 1) for i in range(1, n - 1, 2)]
    across = lax.ppermute(across, "tile", pairs + [(j, i) for i, j in pairs])
    inside = lax.ppermute(inside, "tile", [(i, i ^ 1) for i in range(n)])

    windows = struct((size + 4 * cols, wide), BF16)
    field = struct((ext, chans), BF16)
    kept = struct((n // 2, taps, chans // n, chans), F32)
    sent = struct((n // 2, taps, chans // n, chans), BF16)
    band = pltpu.VMEM((rows, cols, chans), BF16)
    xs, cs, hid, slope, acc = call(
        inner_kernel,
        (in_hbm(f), in_hbm(c), in_hbm(w_two), w_one),
        (windows, windows, field, field, struct((3, chans, wide), F32)),
        [band, band, pltpu.VMEM(w_two.shape, BF16), pltpu.SemaphoreType.DMA((3,))],
        work=3 * flops,
        raw=3,
    )
    xs, cs, hid, fac, keep_two, send_two = call(
        functools.partial(edge_kernel, n, order_two, scale),
        (inside, across, w_one, xs, cs, hid, acc),
        (windows, windows, field, struct((2 * cols, chans), F32), kept, sent),
        place=True,
        aliases={4: 0, 5: 1, 6: 2},
    )
    slope, keep_one, send_one = call(
        functools.partial(terms_kernel, n, order_one, scale),
        (xs, cs, fac, w_two, slope),
        (field, kept, sent),
        place=True,
        aliases={5: 0},
    )
    all_rows = pltpu.VMEM((ext, wide), BF16)
    hid, slope = call(
        functools.partial(sides_kernel, n, cols),
        (xs, cs, w_one, w_two, hid, slope),
        (field, field),
        place=True,
        aliases={5: 0, 6: 1},
    )
    (block_out,) = call(block_kernel, (hid, w_two, f), (struct(f.shape, BF16),), [all_rows])
    (input_grad,) = call(input_kernel, (slope, w_one, c), (struct(c.shape, BF16),), [all_rows])
    grad_two = halve(keep_two, send_two, order_two, n)
    grad_one = halve(keep_one, send_one, order_one, n)
    return (block_out[None], input_grad[None], grad_one, grad_two)


def solution(mesh):
    in_specs = (P("groups", "tile", None, None), P("groups", "tile", None, None), P(), P())
    out_specs = (
        P("groups", "tile", None, None),
        P("groups", "tile", None, None),
        P("tile", "groups", None),
        P("tile", "groups", None),
    )
    return jax.shard_map(layer, mesh=mesh, in_specs=in_specs, out_specs=out_specs, check_vma=False)
```

```python
import functools

import jax
import jax.numpy as jnp
from jax import lax
from jax.experimental import pallas as pl
from jax.experimental.pallas import tpu as pltpu
from jax.sharding import PartitionSpec as P


F32 = jnp.float32
BF16 = jnp.bfloat16
WHOLE = pl.BlockSpec(memory_space=pltpu.VMEM)
LIMIT = 20 << 20
OUTPUT_PARTS = 3


def struct(shape, dtype):
    return jax.ShapeDtypeStruct(shape, dtype)


def pack_kernel(me_ref, f, c, inside, across, sems):
    rows = f.shape[0]
    odd = (me_ref[0] & 1) == 1
    low, high = jnp.where(odd, 0, rows - 2), jnp.where(odd, rows - 2, 0)
    copies = []
    for out, row in ((across, high), (inside, low)):
        for k, field in enumerate((f, c)):
            copies.append(
                pltpu.make_async_copy(
                    field.at[pl.ds(row, 2)], out.at[pl.ds(2 * k, 2)], sems.at[len(copies)]
                )
            )
    for copy in copies:
        copy.start()
    for copy in copies:
        copy.wait()


def in_hbm(array):
    return pltpu.with_memory_space_constraint(array, pltpu.HBM)


def pack(me, features, cotangent):
    out = struct((4,) + features.shape[1:], BF16)
    hbm = pl.BlockSpec(memory_space=pltpu.HBM)
    return pl.pallas_call(
        pack_kernel,
        out_shape=(out,) * 2,
        in_specs=[pl.BlockSpec(memory_space=pltpu.SMEM), hbm, hbm],
        out_specs=(WHOLE,) * 2,
        scratch_shapes=[pltpu.SemaphoreType.DMA((4,))],
        compiler_params=pltpu.CompilerParams(vmem_limit_bytes=8 << 20),
    )(me, in_hbm(features), in_hbm(cotangent))


def put_windows(dst, row, value, sign):
    cols, chans = value.shape
    wide = value.astype(F32)
    index = lax.broadcasted_iota(jnp.int32, (cols, chans), 0)
    before = jnp.where(index == 0, 0.0, pltpu.roll(wide, 1, 0)).astype(BF16)
    after = jnp.where(index == cols - 1, 0.0, pltpu.roll(wide, cols - 1, 0)).astype(BF16)
    here = pl.ds(pl.multiple_of(row * cols, cols), cols)
    low, high = (before, after) if sign > 0 else (after, before)
    dst[here, 0:chans] = low
    dst[here, chans : 2 * chans] = value
    dst[here, 2 * chans : 3 * chans] = high


def fill(dst, base, count, source, first, sign):
    def step(k, carry):
        put_windows(dst, base + k, source[first + k], sign)
        return carry

    lax.fori_loop(0, count, step, 0)


def conv_rows(win, weight, start, size, cols):
    left = jnp.concatenate(
        [win[pl.ds(pl.multiple_of(start + a * cols, cols), size), :] for a in range(3)], axis=1
    )
    return jnp.dot(left, weight[...], preferred_element_type=F32)


def conv_t_rows(win, weight, start, size, cols, chans):
    total = None
    for a in range(3):
        left = win[pl.ds(pl.multiple_of(start + (2 - a) * cols, cols), size), :]
        for b in range(3):
            tap = (a * 3 + b) * chans
            part = lax.dot_general(
                left[:, b * chans : (b + 1) * chans],
                weight[tap : tap + chans, :],
                (((1,), (1,)), ((), ())),
                preferred_element_type=F32,
            )
            total = part if total is None else total + part
    return total


def bit_order(order):
    bits = [b for b in order[1:]]
    return bits


def slot_static(j, bits):
    s = 0
    for b in bits:
        s = s * 2 + ((j >> b) & 1)
    return s


def slot_dynamic(me, bits):
    s = jnp.int32(0)
    for b in bits:
        s = s * 2 + ((me >> b) & 1)
    return s


def store_terms(tap, value, keep, send, me, n, order, scale):
    rows = value.shape[0] // n
    value = value * scale
    bits = bit_order(order)
    mine = slot_dynamic(me, bits)
    flip = ((me >> order[0]) & 1) == 1
    for j in range(n):
        if (j >> order[0]) & 1:
            continue
        other = j ^ (1 << order[0])
        low = value[j * rows : (j + 1) * rows]
        high = value[other * rows : (other + 1) * rows]
        slot = slot_static(j, bits) ^ mine
        keep[slot, tap] = jnp.where(flip, high, low)
        send[slot, tap] = jnp.where(flip, low, high).astype(BF16)


def transposed_dot(left, right):
    return lax.dot_general(left, right, (((0,), (0,)), ((), ())), preferred_element_type=F32)


def rows_of(ref, first, count, cols):
    return ref[first * cols : (first + count) * cols, :]


def pair(ref, one, two, cols):
    return jnp.concatenate([rows_of(ref, one, 1, cols), rows_of(ref, two, 1, cols)], axis=0)


def pre_of_pair(xs, w, one, two, cols):
    left = [pair(xs, one + 1 + a, two + 1 + a, cols) for a in range(3)]
    return jnp.dot(jnp.concatenate(left, axis=1), w[...], preferred_element_type=F32)


def grad_of_pair(cs, w, one, two, cols):
    total = None
    for a in range(3):
        left = pair(cs, one + 3 - a, two + 3 - a, cols)
        chans = left.shape[1] // 3
        for b in range(3):
            tap = (a * 3 + b) * chans
            part = lax.dot_general(
                left[:, b * chans : (b + 1) * chans],
                w[tap : tap + chans, :],
                (((1,), (1,)), ((), ())),
                preferred_element_type=F32,
            )
            total = part if total is None else total + part
    return total


def derivative(pre, sigma):
    return sigma * (1.0 + pre * (1.0 - sigma))


def inner_kernel(f_hbm, c_hbm, w_hbm, w_one, xs, cs, hid, slope, acc, f, c, w_two, sems):
    rows, cols, chans = f.shape
    copy_f = pltpu.make_async_copy(f_hbm, f, sems.at[0])
    copy_c = pltpu.make_async_copy(c_hbm, c, sems.at[1])
    copy_w = pltpu.make_async_copy(w_hbm, w_two, sems.at[2])
    copy_f.start()
    copy_c.start()
    copy_w.start()
    copy_f.wait()
    fill(xs, 2, rows, f, 0, 1)
    copy_c.wait()
    fill(cs, 2, rows, c, 0, -1)
    copy_w.wait()
    half = (rows - 2) // 2
    size = half * cols

    for k in range(2):
        start = (2 + k * half) * cols
        here = pl.ds(pl.multiple_of(start, cols), size)
        pre = conv_rows(xs, w_one, start, size, cols)
        sigma = jax.nn.sigmoid(pre)
        hid[here, :] = (pre * sigma).astype(BF16)
        grad = conv_t_rows(cs, w_two, start, size, cols, chans)
        slope[here, :] = (grad * derivative(pre, sigma)).astype(BF16)
    left = rows_of(hid, 2, rows - 2, cols)
    for a in range(3):
        acc[a] = transposed_dot(left, rows_of(cs, 4 - a, rows - 2, cols))


def edge_kernel(n, order, scale, me_ref, inside, across, w, xs_in, cs_in, hid_in, acc,
                xs, cs, hid, fac, keep, send):
    cols, chans = inside.shape[1:]
    rows = xs.shape[0] // cols - 4
    me = me_ref[0]
    odd = (me & 1) == 1
    for k in range(2):
        for dst, part, sign in ((xs, k, 1), (cs, 2 + k, -1)):
            one, two = inside[part], across[part]
            above, below = jnp.where(odd, one, two), jnp.where(odd, two, one)
            put_windows(dst, k, jnp.where(me == 0, 0.0, above).astype(BF16), sign)
            put_windows(dst, rows + 2 + k, jnp.where(me == n - 1, 0.0, below).astype(BF16), sign)
    pre = pre_of_pair(xs, w, 0, rows - 1, cols)
    sigma = jax.nn.sigmoid(pre)
    hidden = (pre * sigma).astype(BF16)
    hid[cols : 2 * cols, :] = hidden[:cols]
    hid[rows * cols : (rows + 1) * cols, :] = hidden[cols:]
    fac[...] = derivative(pre, sigma)
    left = pair(hid, 1, rows, cols)

    def part(a, carry):
        two = [
            cs[pl.ds(pl.multiple_of((first - a) * cols, cols), cols), :] for first in (3, rows + 2)
        ]
        out = acc[a] + transposed_dot(left, jnp.concatenate(two, axis=0))
        for b in range(3):
            store_terms(
                a * 3 + b, out[:, b * chans : (b + 1) * chans], keep, send, me, n, order, scale
            )
        return carry

    lax.fori_loop(0, 3, part, 0)


def terms_kernel(n, order, scale, me_ref, xs, cs, fac, w, slope_in, slope, keep, send):
    chans = slope.shape[1]
    cols = fac.shape[0] // 2
    rows = xs.shape[0] // cols - 4
    value = (grad_of_pair(cs, w, 0, rows - 1, cols) * fac[...]).astype(BF16)
    slope[cols : 2 * cols, :] = value[:cols]
    slope[rows * cols : (rows + 1) * cols, :] = value[cols:]
    right = rows_of(slope, 1, rows, cols)
    for a in range(3):
        out = transposed_dot(rows_of(xs, 1 + a, rows, cols), right)
        for b in range(3):
            store_terms(
                a * 3 + b, out[b * chans : (b + 1) * chans], keep, send, me_ref[0], n, order, scale
            )


def sides_kernel(n, cols, me_ref, xs, cs, w_one, w_two, hid_in, slope_in, hid, slope):
    rows = xs.shape[0] // cols - 4
    pre = pre_of_pair(xs, w_one, -1, rows, cols)
    grad = grad_of_pair(cs, w_two, -1, rows, cols)
    sigma = jax.nn.sigmoid(pre)
    hidden = pre * sigma
    value = grad * derivative(pre, sigma)
    for side, outside in ((0, me_ref[0] == 0), (1, me_ref[0] == n - 1)):
        here = slice(side * cols, (side + 1) * cols)
        there = slice(side * (rows + 1) * cols, (side * (rows + 1) + 1) * cols)
        hid[there, :] = jnp.where(outside, 0.0, hidden[here]).astype(BF16)
        slope[there, :] = jnp.where(outside, 0.0, value[here]).astype(BF16)


def outputs_kernel(first, hid, slope, xs, cs, w_two, w_one, *refs):
    block_out, input_grad, hs, ss, f_done, c_done, sems = refs[-7:]
    count, cols, chans = f_done.shape
    here = pl.ds(first, count)

    def step(k, carry):
        row = pl.ds(pl.multiple_of((first + k) * cols, cols), cols)
        put_windows(hs, k, hid[row, :], 1)
        put_windows(ss, k, slope[row, :], -1)
        return carry

    lax.fori_loop(0, count + 2, step, 0)
    own = slice((first + 2) * cols, (first + 2 + count) * cols)
    shape = (count, cols, chans)
    total = xs[own, chans : 2 * chans].astype(F32) + conv_rows(hs, w_two, 0, count * cols, cols)
    f_done[...] = total.astype(BF16).reshape(shape)
    store_f = pltpu.make_async_copy(f_done, block_out.at[here], sems.at[0])
    store_f.start()
    grad = conv_t_rows(ss, w_one, 0, count * cols, cols, chans)
    total = cs[own, chans : 2 * chans].astype(F32) + grad
    c_done[...] = total.astype(BF16).reshape(shape)
    store_c = pltpu.make_async_copy(c_done, input_grad.at[here], sems.at[1])
    store_c.start()
    store_f.wait()
    store_c.wait()


def halve(keep, send, order, n):
    for bit in order:
        pairs = [(i, i ^ (1 << bit)) for i in range(n)]
        got = lax.ppermute(send, "tile", pairs)
        total = keep + got.astype(F32)
        half = total.shape[0] // 2
        if half:
            keep, send = total[:half], total[half:].astype(BF16)
        else:
            return jnp.swapaxes(total[0], 0, 1)


def layer(features, cotangent, weight_one, weight_two):
    _, rows, cols, chans = features.shape
    n = lax.axis_size("tile")
    scale = float(rows * n * cols) ** (-0.5)
    me = lax.axis_index("tile").astype(jnp.int32).reshape(1)
    f, c = features[0], cotangent[0]
    taps = weight_one.shape[1]
    w_one = jnp.swapaxes(weight_one, 0, 1).reshape(taps * chans, chans)
    w_two = jnp.swapaxes(weight_two, 0, 1).reshape(taps * chans, chans)

    bits = n.bit_length() - 1
    order_two = list(range(bits))
    order_one = [0, 2, 1] + list(range(3, bits)) if bits > 2 else order_two
    size, ext, wide = rows * cols, (rows + 2) * cols, 3 * chans
    flops = 2 * 9 * size * chans * chans
    smem = pl.BlockSpec(memory_space=pltpu.SMEM)

    hbm = pl.BlockSpec(memory_space=pltpu.HBM)

    def call(kernel, args, outs, scratch=(), work=flops, place=False, aliases={}, raw=0):
        specs = ([smem] if place else []) + [hbm] * raw + [WHOLE] * (len(args) - raw)
        return pl.pallas_call(
            kernel,
            out_shape=outs,
            in_specs=specs,
            out_specs=tuple(WHOLE for _ in outs),
            scratch_shapes=list(scratch),
            input_output_aliases=aliases,
            compiler_params=pltpu.CompilerParams(vmem_limit_bytes=LIMIT),
            cost_estimate=pl.CostEstimate(flops=work, bytes_accessed=4 << 20, transcendentals=0),
        )(*(((me,) if place else ()) + tuple(args)))

    inside, across = pack(me, f, c)
    pairs = [(i, (i + 1) % n) for i in range(1, n, 2)]
    across = lax.ppermute(across, "tile", pairs + [(j, i) for i, j in pairs])
    inside = lax.ppermute(inside, "tile", [(i, i ^ 1) for i in range(n)])

    windows = struct((size + 4 * cols, wide), BF16)
    field = struct((ext, chans), BF16)
    kept = struct((n // 2, taps, chans // n, chans), F32)
    sent = struct((n // 2, taps, chans // n, chans), BF16)
    band = pltpu.VMEM((rows, cols, chans), BF16)
    xs, cs, hid, slope, acc = call(
        inner_kernel,
        (in_hbm(f), in_hbm(c), in_hbm(w_two), w_one),
        (windows, windows, field, field, struct((3, chans, wide), F32)),
        [band, band, pltpu.VMEM(w_two.shape, BF16), pltpu.SemaphoreType.DMA((3,))],
        work=3 * flops,
        raw=3,
    )
    xs, cs, hid, fac, keep_two, send_two = call(
        functools.partial(edge_kernel, n, order_two, scale),
        (inside, across, w_one, xs, cs, hid, acc),
        (windows, windows, field, struct((2 * cols, chans), F32), kept, sent),
        place=True,
        aliases={4: 0, 5: 1, 6: 2},
    )
    slope, keep_one, send_one = call(
        functools.partial(terms_kernel, n, order_one, scale),
        (xs, cs, fac, w_two, slope),
        (field, kept, sent),
        place=True,
        aliases={5: 0},
    )
    hid, slope = call(
        functools.partial(sides_kernel, n, cols),
        (xs, cs, w_one, w_two, hid, slope),
        (field, field),
        place=True,
        aliases={5: 0, 6: 1},
    )
    parts = OUTPUT_PARTS if rows % OUTPUT_PARTS == 0 else 1
    count = rows // parts
    outs = ()
    for part in range(parts):
        outs = pl.pallas_call(
            functools.partial(outputs_kernel, part * count),
            out_shape=(struct(f.shape, BF16), struct(c.shape, BF16)),
            in_specs=[WHOLE] * 6 + [hbm] * len(outs),
            out_specs=(hbm, hbm),
            scratch_shapes=[pltpu.VMEM(((count + 2) * cols, wide), BF16)] * 2
            + [pltpu.VMEM((count, cols, chans), BF16)] * 2
            + [pltpu.SemaphoreType.DMA((2,))],
            input_output_aliases={6: 0, 7: 1} if outs else {},
            compiler_params=pltpu.CompilerParams(vmem_limit_bytes=LIMIT),
            cost_estimate=pl.CostEstimate(
                flops=2 * flops // parts, bytes_accessed=4 << 20, transcendentals=0
            ),
        )(hid, slope, xs, cs, w_two, w_one, *outs)
    block_out, input_grad = outs
    grad_two = halve(keep_two, send_two, order_two, n)
    grad_one = halve(keep_one, send_one, order_one, n)
    return (block_out[None], input_grad[None], grad_one, grad_two)


def solution(mesh):
    in_specs = (P("groups", "tile", None, None), P("groups", "tile", None, None), P(), P())
    out_specs = (
        P("groups", "tile", None, None),
        P("groups", "tile", None, None),
        P("tile", "groups", None),
        P("tile", "groups", None),
    )
    return jax.shard_map(layer, mesh=mesh, in_specs=in_specs, out_specs=out_specs, check_vma=False)
```

```python
import functools

import jax
import jax.numpy as jnp
from jax import lax
from jax.experimental import pallas as pl
from jax.experimental.pallas import tpu as pltpu
from jax.sharding import PartitionSpec as P


F32 = jnp.float32
BF16 = jnp.bfloat16
WHOLE = pl.BlockSpec(memory_space=pltpu.VMEM)
LIMIT = 20 << 20
OUTPUT_PARTS = 4


def struct(shape, dtype):
    return jax.ShapeDtypeStruct(shape, dtype)


def pack_kernel(me_ref, f, c, inside, across, sems):
    rows = f.shape[0]
    odd = (me_ref[0] & 1) == 1
    low, high = jnp.where(odd, 0, rows - 2), jnp.where(odd, rows - 2, 0)
    copies = []
    for out, row in ((across, high), (inside, low)):
        for k, field in enumerate((f, c)):
            copies.append(
                pltpu.make_async_copy(
                    field.at[pl.ds(row, 2)], out.at[pl.ds(2 * k, 2)], sems.at[len(copies)]
                )
            )
    for copy in copies:
        copy.start()
    for copy in copies:
        copy.wait()


def across_pairs(groups, n):
    pairs = []
    for group in range(groups):
        base = group * n
        pairs += [(base + i, base + i + 1) for i in range(1, n - 1, 2)]
        pairs += [(base + i + 1, base + i) for i in range(1, n - 1, 2)]
        twin = (group ^ 1) * n if groups % 2 == 0 else base
        pairs += [(base, twin), (base + n - 1, twin + n - 1)]
    return pairs


def in_hbm(array):
    return pltpu.with_memory_space_constraint(array, pltpu.HBM)


def pack(me, features, cotangent):
    out = struct((4,) + features.shape[1:], BF16)
    hbm = pl.BlockSpec(memory_space=pltpu.HBM)
    return pl.pallas_call(
        pack_kernel,
        out_shape=(out,) * 2,
        in_specs=[pl.BlockSpec(memory_space=pltpu.SMEM), hbm, hbm],
        out_specs=(WHOLE,) * 2,
        scratch_shapes=[pltpu.SemaphoreType.DMA((4,))],
        compiler_params=pltpu.CompilerParams(vmem_limit_bytes=8 << 20),
    )(me, in_hbm(features), in_hbm(cotangent))


def put_windows(dst, row, value, sign):
    cols, chans = value.shape
    wide = value.astype(F32)
    index = lax.broadcasted_iota(jnp.int32, (cols, chans), 0)
    before = jnp.where(index == 0, 0.0, pltpu.roll(wide, 1, 0)).astype(BF16)
    after = jnp.where(index == cols - 1, 0.0, pltpu.roll(wide, cols - 1, 0)).astype(BF16)
    here = pl.ds(pl.multiple_of(row * cols, cols), cols)
    low, high = (before, after) if sign > 0 else (after, before)
    dst[here, 0:chans] = low
    dst[here, chans : 2 * chans] = value
    dst[here, 2 * chans : 3 * chans] = high


def fill(dst, base, count, source, first, sign):
    def step(k, carry):
        put_windows(dst, base + k, source[first + k], sign)
        return carry

    lax.fori_loop(0, count, step, 0)


def conv_rows(win, weight, start, size, cols):
    left = jnp.concatenate(
        [win[pl.ds(pl.multiple_of(start + a * cols, cols), size), :] for a in range(3)], axis=1
    )
    return jnp.dot(left, weight[...], preferred_element_type=F32)


def conv_t_rows(win, weight, start, size, cols, chans):
    total = None
    for a in range(3):
        left = win[pl.ds(pl.multiple_of(start + (2 - a) * cols, cols), size), :]
        for b in range(3):
            tap = (a * 3 + b) * chans
            part = lax.dot_general(
                left[:, b * chans : (b + 1) * chans],
                weight[tap : tap + chans, :],
                (((1,), (1,)), ((), ())),
                preferred_element_type=F32,
            )
            total = part if total is None else total + part
    return total


def bit_order(order):
    bits = [b for b in order[1:]]
    return bits


def slot_static(j, bits):
    s = 0
    for b in bits:
        s = s * 2 + ((j >> b) & 1)
    return s


def slot_dynamic(me, bits):
    s = jnp.int32(0)
    for b in bits:
        s = s * 2 + ((me >> b) & 1)
    return s


def store_terms(tap, value, keep, send, me, n, order, scale):
    rows = value.shape[0] // n
    value = value * scale
    bits = bit_order(order)
    mine = slot_dynamic(me, bits)
    flip = ((me >> order[0]) & 1) == 1
    for j in range(n):
        if (j >> order[0]) & 1:
            continue
        other = j ^ (1 << order[0])
        low = value[j * rows : (j + 1) * rows]
        high = value[other * rows : (other + 1) * rows]
        slot = slot_static(j, bits) ^ mine
        keep[slot, tap] = jnp.where(flip, high, low)
        send[slot, tap] = jnp.where(flip, low, high).astype(BF16)


def transposed_dot(left, right):
    return lax.dot_general(left, right, (((0,), (0,)), ((), ())), preferred_element_type=F32)


def rows_of(ref, first, count, cols):
    return ref[first * cols : (first + count) * cols, :]


def pair(ref, one, two, cols):
    return jnp.concatenate([rows_of(ref, one, 1, cols), rows_of(ref, two, 1, cols)], axis=0)


def pre_of_pair(xs, w, one, two, cols):
    left = [pair(xs, one + 1 + a, two + 1 + a, cols) for a in range(3)]
    return jnp.dot(jnp.concatenate(left, axis=1), w[...], preferred_element_type=F32)


def grad_of_pair(cs, w, one, two, cols):
    total = None
    for a in range(3):
        left = pair(cs, one + 3 - a, two + 3 - a, cols)
        chans = left.shape[1] // 3
        for b in range(3):
            tap = (a * 3 + b) * chans
            part = lax.dot_general(
                left[:, b * chans : (b + 1) * chans],
                w[tap : tap + chans, :],
                (((1,), (1,)), ((), ())),
                preferred_element_type=F32,
            )
            total = part if total is None else total + part
    return total


def derivative(pre, sigma):
    return sigma * (1.0 + pre * (1.0 - sigma))


def inner_kernel(f_hbm, c_hbm, w_hbm, w_one, xs, cs, hid, slope, acc, f, c, w_two, sems):
    rows, cols, chans = f.shape
    copy_f = pltpu.make_async_copy(f_hbm, f, sems.at[0])
    copy_c = pltpu.make_async_copy(c_hbm, c, sems.at[1])
    copy_w = pltpu.make_async_copy(w_hbm, w_two, sems.at[2])
    copy_f.start()
    copy_c.start()
    copy_w.start()
    copy_f.wait()
    fill(xs, 2, rows, f, 0, 1)
    copy_c.wait()
    fill(cs, 2, rows, c, 0, -1)
    copy_w.wait()
    half = (rows - 2) // 2
    size = half * cols

    for k in range(2):
        start = (2 + k * half) * cols
        here = pl.ds(pl.multiple_of(start, cols), size)
        pre = conv_rows(xs, w_one, start, size, cols)
        sigma = jax.nn.sigmoid(pre)
        hid[here, :] = (pre * sigma).astype(BF16)
        grad = conv_t_rows(cs, w_two, start, size, cols, chans)
        slope[here, :] = (grad * derivative(pre, sigma)).astype(BF16)
    left = rows_of(hid, 2, rows - 2, cols)
    for a in range(3):
        acc[a] = transposed_dot(left, rows_of(cs, 4 - a, rows - 2, cols))


def edge_kernel(n, order, scale, me_ref, inside, across, w, xs_in, cs_in, hid_in, acc,
                xs, cs, hid, fac, keep, send):
    cols, chans = inside.shape[1:]
    rows = xs.shape[0] // cols - 4
    me = me_ref[0]
    odd = (me & 1) == 1
    for k in range(2):
        for dst, part, sign in ((xs, k, 1), (cs, 2 + k, -1)):
            one, two = inside[part], across[part]
            above, below = jnp.where(odd, one, two), jnp.where(odd, two, one)
            put_windows(dst, k, jnp.where(me == 0, 0.0, above).astype(BF16), sign)
            put_windows(dst, rows + 2 + k, jnp.where(me == n - 1, 0.0, below).astype(BF16), sign)
    pre = pre_of_pair(xs, w, 0, rows - 1, cols)
    sigma = jax.nn.sigmoid(pre)
    hidden = (pre * sigma).astype(BF16)
    hid[cols : 2 * cols, :] = hidden[:cols]
    hid[rows * cols : (rows + 1) * cols, :] = hidden[cols:]
    fac[...] = derivative(pre, sigma)
    left = pair(hid, 1, rows, cols)

    def part(a, carry):
        two = [
            cs[pl.ds(pl.multiple_of((first - a) * cols, cols), cols), :] for first in (3, rows + 2)
        ]
        out = acc[a] + transposed_dot(left, jnp.concatenate(two, axis=0))
        for b in range(3):
            store_terms(
                a * 3 + b, out[:, b * chans : (b + 1) * chans], keep, send, me, n, order, scale
            )
        return carry

    lax.fori_loop(0, 3, part, 0)


def terms_kernel(n, order, scale, me_ref, xs, cs, fac, w, slope_in, slope, keep, send):
    chans = slope.shape[1]
    cols = fac.shape[0] // 2
    rows = xs.shape[0] // cols - 4
    value = (grad_of_pair(cs, w, 0, rows - 1, cols) * fac[...]).astype(BF16)
    slope[cols : 2 * cols, :] = value[:cols]
    slope[rows * cols : (rows + 1) * cols, :] = value[cols:]
    right = rows_of(slope, 1, rows, cols)
    for a in range(3):
        out = transposed_dot(rows_of(xs, 1 + a, rows, cols), right)
        for b in range(3):
            store_terms(
                a * 3 + b, out[b * chans : (b + 1) * chans], keep, send, me_ref[0], n, order, scale
            )


def sides_kernel(n, cols, me_ref, xs, cs, w_one, w_two, hid_in, slope_in, hid, slope):
    rows = xs.shape[0] // cols - 4
    pre = pre_of_pair(xs, w_one, -1, rows, cols)
    grad = grad_of_pair(cs, w_two, -1, rows, cols)
    sigma = jax.nn.sigmoid(pre)
    hidden = pre * sigma
    value = grad * derivative(pre, sigma)
    for side, outside in ((0, me_ref[0] == 0), (1, me_ref[0] == n - 1)):
        here = slice(side * cols, (side + 1) * cols)
        there = slice(side * (rows + 1) * cols, (side * (rows + 1) + 1) * cols)
        hid[there, :] = jnp.where(outside, 0.0, hidden[here]).astype(BF16)
        slope[there, :] = jnp.where(outside, 0.0, value[here]).astype(BF16)


def outputs_kernel(first, hid, slope, xs, cs, w_two, w_one, *refs):
    block_out, input_grad, hs, ss, f_done, c_done, sems = refs[-7:]
    count, cols, chans = f_done.shape
    here = pl.ds(first, count)

    def step(k, carry):
        row = pl.ds(pl.multiple_of((first + k) * cols, cols), cols)
        put_windows(hs, k, hid[row, :], 1)
        put_windows(ss, k, slope[row, :], -1)
        return carry

    lax.fori_loop(0, count + 2, step, 0)
    own = slice((first + 2) * cols, (first + 2 + count) * cols)
    shape = (count, cols, chans)
    total = xs[own, chans : 2 * chans].astype(F32) + conv_rows(hs, w_two, 0, count * cols, cols)
    f_done[...] = total.astype(BF16).reshape(shape)
    store_f = pltpu.make_async_copy(f_done, block_out.at[here], sems.at[0])
    store_f.start()
    grad = conv_t_rows(ss, w_one, 0, count * cols, cols, chans)
    total = cs[own, chans : 2 * chans].astype(F32) + grad
    c_done[...] = total.astype(BF16).reshape(shape)
    store_c = pltpu.make_async_copy(c_done, input_grad.at[here], sems.at[1])
    store_c.start()
    store_f.wait()
    store_c.wait()


def halve(keep, send, order, n):
    for bit in order:
        pairs = [(i, i ^ (1 << bit)) for i in range(n)]
        got = lax.ppermute(send, "tile", pairs)
        total = keep + got.astype(F32)
        half = total.shape[0] // 2
        if half:
            keep, send = total[:half], total[half:].astype(BF16)
        else:
            return jnp.swapaxes(total[0], 0, 1)


def layer(features, cotangent, weight_one, weight_two):
    _, rows, cols, chans = features.shape
    n = lax.axis_size("tile")
    scale = float(rows * n * cols) ** (-0.5)
    me = lax.axis_index("tile").astype(jnp.int32).reshape(1)
    f, c = features[0], cotangent[0]
    taps = weight_one.shape[1]
    w_one = jnp.swapaxes(weight_one, 0, 1).reshape(taps * chans, chans)
    w_two = jnp.swapaxes(weight_two, 0, 1).reshape(taps * chans, chans)

    bits = n.bit_length() - 1
    order_two = list(range(bits))
    order_one = [0, 2, 1] + list(range(3, bits)) if bits > 2 else order_two
    size, ext, wide = rows * cols, (rows + 2) * cols, 3 * chans
    flops = 2 * 9 * size * chans * chans
    smem = pl.BlockSpec(memory_space=pltpu.SMEM)

    hbm = pl.BlockSpec(memory_space=pltpu.HBM)

    def call(kernel, args, outs, scratch=(), work=flops, place=False, aliases={}, raw=0):
        specs = ([smem] if place else []) + [hbm] * raw + [WHOLE] * (len(args) - raw)
        return pl.pallas_call(
            kernel,
            out_shape=outs,
            in_specs=specs,
            out_specs=tuple(WHOLE for _ in outs),
            scratch_shapes=list(scratch),
            input_output_aliases=aliases,
            compiler_params=pltpu.CompilerParams(vmem_limit_bytes=LIMIT),
            cost_estimate=pl.CostEstimate(flops=work, bytes_accessed=4 << 20, transcendentals=0),
        )(*(((me,) if place else ()) + tuple(args)))

    inside, across = pack(me, f, c)
    across = lax.ppermute(across, ("groups", "tile"), across_pairs(lax.axis_size("groups"), n))
    inside = lax.ppermute(inside, "tile", [(i, i ^ 1) for i in range(n)])

    windows = struct((size + 4 * cols, wide), BF16)
    field = struct((ext, chans), BF16)
    kept = struct((n // 2, taps, chans // n, chans), F32)
    sent = struct((n // 2, taps, chans // n, chans), BF16)
    band = pltpu.VMEM((rows, cols, chans), BF16)
    xs, cs, hid, slope, acc = call(
        inner_kernel,
        (in_hbm(f), in_hbm(c), in_hbm(w_two), w_one),
        (windows, windows, field, field, struct((3, chans, wide), F32)),
        [band, band, pltpu.VMEM(w_two.shape, BF16), pltpu.SemaphoreType.DMA((3,))],
        work=3 * flops,
        raw=3,
    )
    xs, cs, hid, fac, keep_two, send_two = call(
        functools.partial(edge_kernel, n, order_two, scale),
        (inside, across, w_one, xs, cs, hid, acc),
        (windows, windows, field, struct((2 * cols, chans), F32), kept, sent),
        place=True,
        aliases={4: 0, 5: 1, 6: 2},
    )
    slope, keep_one, send_one = call(
        functools.partial(terms_kernel, n, order_one, scale),
        (xs, cs, fac, w_two, slope),
        (field, kept, sent),
        place=True,
        aliases={5: 0},
    )
    hid, slope = call(
        functools.partial(sides_kernel, n, cols),
        (xs, cs, w_one, w_two, hid, slope),
        (field, field),
        place=True,
        aliases={5: 0, 6: 1},
    )
    parts = OUTPUT_PARTS if rows % OUTPUT_PARTS == 0 else 1
    count = rows // parts
    outs = ()
    for part in range(parts):
        outs = pl.pallas_call(
            functools.partial(outputs_kernel, part * count),
            out_shape=(struct(f.shape, BF16), struct(c.shape, BF16)),
            in_specs=[WHOLE] * 6 + [hbm] * len(outs),
            out_specs=(hbm, hbm),
            scratch_shapes=[pltpu.VMEM(((count + 2) * cols, wide), BF16)] * 2
            + [pltpu.VMEM((count, cols, chans), BF16)] * 2
            + [pltpu.SemaphoreType.DMA((2,))],
            input_output_aliases={6: 0, 7: 1} if outs else {},
            compiler_params=pltpu.CompilerParams(vmem_limit_bytes=LIMIT),
            cost_estimate=pl.CostEstimate(
                flops=2 * flops // parts, bytes_accessed=4 << 20, transcendentals=0
            ),
        )(hid, slope, xs, cs, w_two, w_one, *outs)
    block_out, input_grad = outs
    grad_two = halve(keep_two, send_two, order_two, n)
    grad_one = halve(keep_one, send_one, order_one, n)
    return (block_out[None], input_grad[None], grad_one, grad_two)


def solution(mesh):
    in_specs = (P("groups", "tile", None, None), P("groups", "tile", None, None), P(), P())
    out_specs = (
        P("groups", "tile", None, None),
        P("groups", "tile", None, None),
        P("tile", "groups", None),
        P("tile", "groups", None),
    )
    return jax.shard_map(layer, mesh=mesh, in_specs=in_specs, out_specs=out_specs, check_vma=False)
```

```python
import functools

import jax
import jax.numpy as jnp
from jax import lax
from jax.experimental import pallas as pl
from jax.experimental.pallas import tpu as pltpu
from jax.sharding import PartitionSpec as P


F32 = jnp.float32
BF16 = jnp.bfloat16
WHOLE = pl.BlockSpec(memory_space=pltpu.VMEM)
LIMIT = 20 << 20
SHARES = (6, 6)
PIECES = 4


def struct(shape, dtype):
    return jax.ShapeDtypeStruct(shape, dtype)


def pack_kernel(me_ref, f, c, inside, across, sems):
    rows = f.shape[0]
    odd = (me_ref[0] & 1) == 1
    low, high = jnp.where(odd, 0, rows - 2), jnp.where(odd, rows - 2, 0)
    copies = []
    for out, row in ((across, high), (inside, low)):
        for k, field in enumerate((f, c)):
            copies.append(
                pltpu.make_async_copy(
                    field.at[pl.ds(row, 2)], out.at[pl.ds(2 * k, 2)], sems.at[len(copies)]
                )
            )
    for copy in copies:
        copy.start()
    for copy in copies:
        copy.wait()


def across_pairs(groups, n):
    pairs = []
    for group in range(groups):
        base = group * n
        pairs += [(base + i, base + i + 1) for i in range(1, n - 1, 2)]
        pairs += [(base + i + 1, base + i) for i in range(1, n - 1, 2)]
        twin = (group ^ 1) * n if groups % 2 == 0 else base
        pairs += [(base, twin), (base + n - 1, twin + n - 1)]
    return pairs


def in_hbm(array):
    return pltpu.with_memory_space_constraint(array, pltpu.HBM)


def pack(me, features, cotangent):
    out = struct((4,) + features.shape[1:], BF16)
    hbm = pl.BlockSpec(memory_space=pltpu.HBM)
    return pl.pallas_call(
        pack_kernel,
        out_shape=(out,) * 2,
        in_specs=[pl.BlockSpec(memory_space=pltpu.SMEM), hbm, hbm],
        out_specs=(WHOLE,) * 2,
        scratch_shapes=[pltpu.SemaphoreType.DMA((4,))],
        compiler_params=pltpu.CompilerParams(vmem_limit_bytes=8 << 20),
    )(me, in_hbm(features), in_hbm(cotangent))


def put_windows(dst, row, value, sign):
    cols, chans = value.shape
    zero = jnp.zeros((1, chans), value.dtype)
    before = jnp.concatenate([zero, value[: cols - 1]], axis=0)
    after = jnp.concatenate([value[1:], zero], axis=0)
    here = pl.ds(pl.multiple_of(row * cols, cols), cols)
    low, high = (before, after) if sign > 0 else (after, before)
    dst[here, 0:chans] = low
    dst[here, chans : 2 * chans] = value
    dst[here, 2 * chans : 3 * chans] = high


def fill(dst, base, count, source, first, sign):
    def step(k, carry):
        put_windows(dst, base + k, source[first + k], sign)
        return carry

    lax.fori_loop(0, count, step, 0)


def conv_rows(win, weight, start, size, cols):
    left = jnp.concatenate(
        [win[pl.ds(pl.multiple_of(start + a * cols, cols), size), :] for a in range(3)], axis=1
    )
    return jnp.dot(left, weight[...], preferred_element_type=F32)


def conv_t_rows(win, weight, start, size, cols, chans):
    total = None
    for a in range(3):
        left = win[pl.ds(pl.multiple_of(start + (2 - a) * cols, cols), size), :]
        for b in range(3):
            tap = (a * 3 + b) * chans
            part = lax.dot_general(
                left[:, b * chans : (b + 1) * chans],
                weight[tap : tap + chans, :],
                (((1,), (1,)), ((), ())),
                preferred_element_type=F32,
            )
            total = part if total is None else total + part
    return total


def bit_order(order):
    bits = [b for b in order[1:]]
    return bits


def slot_static(j, bits):
    s = 0
    for b in bits:
        s = s * 2 + ((j >> b) & 1)
    return s


def slot_dynamic(me, bits):
    s = jnp.int32(0)
    for b in bits:
        s = s * 2 + ((me >> b) & 1)
    return s


def store_terms(tap, value, keep, send, me, n, order, scale):
    rows = value.shape[0] // n
    value = value * scale
    bits = bit_order(order)
    mine = slot_dynamic(me, bits)
    flip = ((me >> order[0]) & 1) == 1
    for j in range(n):
        if (j >> order[0]) & 1:
            continue
        other = j ^ (1 << order[0])
        low = value[j * rows : (j + 1) * rows]
        high = value[other * rows : (other + 1) * rows]
        slot = slot_static(j, bits) ^ mine
        keep[slot, tap] = jnp.where(flip, high, low)
        send[slot, tap] = jnp.where(flip, low, high).astype(BF16)


def transposed_dot(left, right):
    return lax.dot_general(left, right, (((0,), (0,)), ((), ())), preferred_element_type=F32)


def rows_of(ref, first, count, cols):
    return ref[first * cols : (first + count) * cols, :]


def pair(ref, one, two, cols):
    return jnp.concatenate([rows_of(ref, one, 1, cols), rows_of(ref, two, 1, cols)], axis=0)


def pre_of_pair(xs, w, one, two, cols):
    left = [pair(xs, one + 1 + a, two + 1 + a, cols) for a in range(3)]
    return jnp.dot(jnp.concatenate(left, axis=1), w[...], preferred_element_type=F32)


def grad_of_pair(cs, w, one, two, cols):
    total = None
    for a in range(3):
        left = pair(cs, one + 3 - a, two + 3 - a, cols)
        chans = left.shape[1] // 3
        for b in range(3):
            tap = (a * 3 + b) * chans
            part = lax.dot_general(
                left[:, b * chans : (b + 1) * chans],
                w[tap : tap + chans, :],
                (((1,), (1,)), ((), ())),
                preferred_element_type=F32,
            )
            total = part if total is None else total + part
    return total


def derivative(pre, sigma):
    return sigma * (1.0 + pre * (1.0 - sigma))


def inner_kernel(f_hbm, c_hbm, w_hbm, w_one, xs, cs, hid, slope, acc, f, c, w_two, sems):
    rows, cols, chans = f.shape
    loads = []
    for slot, (source, target) in enumerate(((f_hbm, f), (c_hbm, c), (w_hbm, w_two))):
        piece = target.shape[0] // PIECES
        loads.append([
            pltpu.make_async_copy(
                source.at[pl.ds(j * piece, piece)],
                target.at[pl.ds(j * piece, piece)],
                sems.at[slot * PIECES + j],
            )
            for j in range(PIECES)
        ])
    for group in loads:
        for load in group:
            load.start()
    for dst, field, group, sign in ((xs, f, loads[0], 1), (cs, c, loads[1], -1)):
        piece = rows // PIECES
        for j, load in enumerate(group):
            load.wait()
            fill(dst, 2 + j * piece, piece, field, j * piece, sign)
    for load in loads[2]:
        load.wait()
    half = (rows - 2) // 2
    size = half * cols

    for k in range(2):
        start = (2 + k * half) * cols
        here = pl.ds(pl.multiple_of(start, cols), size)
        pre = conv_rows(xs, w_one, start, size, cols)
        sigma = jax.nn.sigmoid(pre)
        hid[here, :] = (pre * sigma).astype(BF16)
        grad = conv_t_rows(cs, w_two, start, size, cols, chans)
        slope[here, :] = (grad * derivative(pre, sigma)).astype(BF16)
    left = rows_of(hid, 2, rows - 2, cols)
    for a in range(3):
        acc[a] = transposed_dot(left, rows_of(cs, 4 - a, rows - 2, cols))


def edge_kernel(n, order, scale, me_ref, inside, across, w, xs_in, cs_in, hid_in, acc,
                xs, cs, hid, fac, keep, send):
    cols, chans = inside.shape[1:]
    rows = xs.shape[0] // cols - 4
    me = me_ref[0]
    odd = (me & 1) == 1
    for k in range(2):
        for dst, part, sign in ((xs, k, 1), (cs, 2 + k, -1)):
            one, two = inside[part], across[part]
            above, below = jnp.where(odd, one, two), jnp.where(odd, two, one)
            put_windows(dst, k, jnp.where(me == 0, 0.0, above).astype(BF16), sign)
            put_windows(dst, rows + 2 + k, jnp.where(me == n - 1, 0.0, below).astype(BF16), sign)
    pre = pre_of_pair(xs, w, 0, rows - 1, cols)
    sigma = jax.nn.sigmoid(pre)
    hidden = (pre * sigma).astype(BF16)
    hid[cols : 2 * cols, :] = hidden[:cols]
    hid[rows * cols : (rows + 1) * cols, :] = hidden[cols:]
    fac[...] = derivative(pre, sigma)
    left = pair(hid, 1, rows, cols)

    def part(a, carry):
        two = [
            cs[pl.ds(pl.multiple_of((first - a) * cols, cols), cols), :] for first in (3, rows + 2)
        ]
        out = acc[a] + transposed_dot(left, jnp.concatenate(two, axis=0))
        for b in range(3):
            store_terms(
                a * 3 + b, out[:, b * chans : (b + 1) * chans], keep, send, me, n, order, scale
            )
        return carry

    lax.fori_loop(0, 3, part, 0)


def terms_kernel(n, order, scale, me_ref, xs, cs, fac, w, slope_in, slope, keep, send):
    chans = slope.shape[1]
    cols = fac.shape[0] // 2
    rows = xs.shape[0] // cols - 4
    value = (grad_of_pair(cs, w, 0, rows - 1, cols) * fac[...]).astype(BF16)
    slope[cols : 2 * cols, :] = value[:cols]
    slope[rows * cols : (rows + 1) * cols, :] = value[cols:]
    right = rows_of(slope, 1, rows, cols)
    for a in range(3):
        out = transposed_dot(rows_of(xs, 1 + a, rows, cols), right)
        for b in range(3):
            store_terms(
                a * 3 + b, out[b * chans : (b + 1) * chans], keep, send, me_ref[0], n, order, scale
            )


def sides_kernel(n, cols, me_ref, xs, cs, w_one, w_two, hid_in, slope_in, hid, slope):
    rows = xs.shape[0] // cols - 4
    pre = pre_of_pair(xs, w_one, -1, rows, cols)
    grad = grad_of_pair(cs, w_two, -1, rows, cols)
    sigma = jax.nn.sigmoid(pre)
    hidden = pre * sigma
    value = grad * derivative(pre, sigma)
    for side, outside in ((0, me_ref[0] == 0), (1, me_ref[0] == n - 1)):
        here = slice(side * cols, (side + 1) * cols)
        there = slice(side * (rows + 1) * cols, (side * (rows + 1) + 1) * cols)
        hid[there, :] = jnp.where(outside, 0.0, hidden[here]).astype(BF16)
        slope[there, :] = jnp.where(outside, 0.0, value[here]).astype(BF16)


def outputs_kernel(first, hid, slope, xs, cs, w_two, w_one, *refs):
    block_out, input_grad, hs, ss, f_done, c_done, sems = refs[-7:]
    count, cols, chans = f_done.shape
    here = pl.ds(first, count)

    def step(k, carry):
        row = pl.ds(pl.multiple_of((first + k) * cols, cols), cols)
        put_windows(hs, k, hid[row, :], 1)
        put_windows(ss, k, slope[row, :], -1)
        return carry

    lax.fori_loop(0, count + 2, step, 0)
    own = slice((first + 2) * cols, (first + 2 + count) * cols)
    shape = (count, cols, chans)
    total = xs[own, chans : 2 * chans].astype(F32) + conv_rows(hs, w_two, 0, count * cols, cols)
    f_done[...] = total.astype(BF16).reshape(shape)
    store_f = pltpu.make_async_copy(f_done, block_out.at[here], sems.at[0])
    store_f.start()
    grad = conv_t_rows(ss, w_one, 0, count * cols, cols, chans)
    total = cs[own, chans : 2 * chans].astype(F32) + grad
    c_done[...] = total.astype(BF16).reshape(shape)
    store_c = pltpu.make_async_copy(c_done, input_grad.at[here], sems.at[1])
    store_c.start()
    store_f.wait()
    store_c.wait()


def halve(keep, send, order, n):
    for bit in order:
        pairs = [(i, i ^ (1 << bit)) for i in range(n)]
        got = lax.ppermute(send, "tile", pairs)
        total = keep + got.astype(F32)
        half = total.shape[0] // 2
        if half:
            keep, send = total[:half], total[half:].astype(BF16)
        else:
            return jnp.swapaxes(total[0], 0, 1)


def layer(features, cotangent, weight_one, weight_two):
    _, rows, cols, chans = features.shape
    n = lax.axis_size("tile")
    scale = float(rows * n * cols) ** (-0.5)
    me = lax.axis_index("tile").astype(jnp.int32).reshape(1)
    f, c = features[0], cotangent[0]
    taps = weight_one.shape[1]
    w_one = jnp.swapaxes(weight_one, 0, 1).reshape(taps * chans, chans)
    w_two = jnp.swapaxes(weight_two, 0, 1).reshape(taps * chans, chans)

    bits = n.bit_length() - 1
    order_two = list(range(bits))
    order_one = [0, 2, 1] + list(range(3, bits)) if bits > 2 else order_two
    size, ext, wide = rows * cols, (rows + 2) * cols, 3 * chans
    flops = 2 * 9 * size * chans * chans
    smem = pl.BlockSpec(memory_space=pltpu.SMEM)

    hbm = pl.BlockSpec(memory_space=pltpu.HBM)

    def call(kernel, args, outs, scratch=(), work=flops, place=False, aliases={}, raw=0):
        specs = ([smem] if place else []) + [hbm] * raw + [WHOLE] * (len(args) - raw)
        return pl.pallas_call(
            kernel,
            out_shape=outs,
            in_specs=specs,
            out_specs=tuple(WHOLE for _ in outs),
            scratch_shapes=list(scratch),
            input_output_aliases=aliases,
            compiler_params=pltpu.CompilerParams(vmem_limit_bytes=LIMIT),
            cost_estimate=pl.CostEstimate(flops=work, bytes_accessed=4 << 20, transcendentals=0),
        )(*(((me,) if place else ()) + tuple(args)))

    inside, across = pack(me, f, c)
    across = lax.ppermute(across, ("groups", "tile"), across_pairs(lax.axis_size("groups"), n))
    inside = lax.ppermute(inside, "tile", [(i, i ^ 1) for i in range(n)])

    windows = struct((size + 4 * cols, wide), BF16)
    field = struct((ext, chans), BF16)
    kept = struct((n // 2, taps, chans // n, chans), F32)
    sent = struct((n // 2, taps, chans // n, chans), BF16)
    band = pltpu.VMEM((rows, cols, chans), BF16)
    xs, cs, hid, slope, acc = call(
        inner_kernel,
        (in_hbm(f), in_hbm(c), in_hbm(w_two), w_one),
        (windows, windows, field, field, struct((3, chans, wide), F32)),
        [band, band, pltpu.VMEM(w_two.shape, BF16), pltpu.SemaphoreType.DMA((3 * PIECES,))],
        work=3 * flops,
        raw=3,
    )
    xs, cs, hid, fac, keep_two, send_two = call(
        functools.partial(edge_kernel, n, order_two, scale),
        (inside, across, w_one, xs, cs, hid, acc),
        (windows, windows, field, struct((2 * cols, chans), F32), kept, sent),
        place=True,
        aliases={4: 0, 5: 1, 6: 2},
    )
    slope, keep_one, send_one = call(
        functools.partial(terms_kernel, n, order_one, scale),
        (xs, cs, fac, w_two, slope),
        (field, kept, sent),
        place=True,
        aliases={5: 0},
    )
    hid, slope = call(
        functools.partial(sides_kernel, n, cols),
        (xs, cs, w_one, w_two, hid, slope),
        (field, field),
        place=True,
        aliases={5: 0, 6: 1},
    )
    shares = [rows * share // sum(SHARES) for share in SHARES]
    shares[-1] = rows - sum(shares[:-1])
    outs, first = (), 0
    for count in shares:
        outs = pl.pallas_call(
            functools.partial(outputs_kernel, first),
            out_shape=(struct(f.shape, BF16), struct(c.shape, BF16)),
            in_specs=[WHOLE] * 6 + [hbm] * len(outs),
            out_specs=(hbm, hbm),
            scratch_shapes=[pltpu.VMEM(((count + 2) * cols, wide), BF16)] * 2
            + [pltpu.VMEM((count, cols, chans), BF16)] * 2
            + [pltpu.SemaphoreType.DMA((2,))],
            input_output_aliases={6: 0, 7: 1} if outs else {},
            compiler_params=pltpu.CompilerParams(vmem_limit_bytes=LIMIT),
            cost_estimate=pl.CostEstimate(
                flops=2 * flops * count // rows, bytes_accessed=4 << 20, transcendentals=0
            ),
        )(hid, slope, xs, cs, w_two, w_one, *outs)
        first += count
    block_out, input_grad = outs
    grad_two = halve(keep_two, send_two, order_two, n)
    grad_one = halve(keep_one, send_one, order_one, n)
    return (block_out[None], input_grad[None], grad_one, grad_two)


def solution(mesh):
    in_specs = (P("groups", "tile", None, None), P("groups", "tile", None, None), P(), P())
    out_specs = (
        P("groups", "tile", None, None),
        P("groups", "tile", None, None),
        P("tile", "groups", None),
        P("tile", "groups", None),
    )
    return jax.shard_map(layer, mesh=mesh, in_specs=in_specs, out_specs=out_specs, check_vma=False)
```

```python
import functools

import jax
import jax.numpy as jnp
from jax import lax
from jax.experimental import pallas as pl
from jax.experimental.pallas import tpu as pltpu
from jax.sharding import PartitionSpec as P


F32 = jnp.float32
BF16 = jnp.bfloat16
WHOLE = pl.BlockSpec(memory_space=pltpu.VMEM)
LIMIT = 20 << 20
SHARES = (6, 6)
PIECES = 4


def struct(shape, dtype):
    return jax.ShapeDtypeStruct(shape, dtype)


def pack_kernel(me_ref, f, c, inside, across, sems):
    rows = f.shape[0]
    odd = (me_ref[0] & 1) == 1
    low, high = jnp.where(odd, 0, rows - 2), jnp.where(odd, rows - 2, 0)
    copies = []
    for out, row in ((across, high), (inside, low)):
        for k, field in enumerate((f, c)):
            copies.append(
                pltpu.make_async_copy(
                    field.at[pl.ds(row, 2)], out.at[pl.ds(2 * k, 2)], sems.at[len(copies)]
                )
            )
    for copy in copies:
        copy.start()
    for copy in copies:
        copy.wait()


def across_pairs(groups, n):
    pairs = []
    for group in range(groups):
        base = group * n
        pairs += [(base + i, base + i + 1) for i in range(1, n - 1, 2)]
        pairs += [(base + i + 1, base + i) for i in range(1, n - 1, 2)]
        twin = (group ^ 1) * n if groups % 2 == 0 else base
        pairs += [(base, twin), (base + n - 1, twin + n - 1)]
    return pairs


def in_hbm(array):
    return pltpu.with_memory_space_constraint(array, pltpu.HBM)


def pack(me, features, cotangent):
    out = struct((4,) + features.shape[1:], BF16)
    hbm = pl.BlockSpec(memory_space=pltpu.HBM)
    return pl.pallas_call(
        pack_kernel,
        out_shape=(out,) * 2,
        in_specs=[pl.BlockSpec(memory_space=pltpu.SMEM), hbm, hbm],
        out_specs=(WHOLE,) * 2,
        scratch_shapes=[pltpu.SemaphoreType.DMA((4,))],
        compiler_params=pltpu.CompilerParams(vmem_limit_bytes=8 << 20),
    )(me, in_hbm(features), in_hbm(cotangent))


def put_windows(dst, row, value, sign):
    cols, chans = value.shape
    zero = jnp.zeros((1, chans), value.dtype)
    before = jnp.concatenate([zero, value[: cols - 1]], axis=0)
    after = jnp.concatenate([value[1:], zero], axis=0)
    here = pl.ds(pl.multiple_of(row * cols, cols), cols)
    low, high = (before, after) if sign > 0 else (after, before)
    dst[here, 0:chans] = low
    dst[here, chans : 2 * chans] = value
    dst[here, 2 * chans : 3 * chans] = high


def fill(dst, base, count, source, first, sign):
    def step(k, carry):
        put_windows(dst, base + k, source[first + k], sign)
        return carry

    lax.fori_loop(0, count, step, 0)


def conv_rows(win, weight, start, size, cols):
    left = jnp.concatenate(
        [win[pl.ds(pl.multiple_of(start + a * cols, cols), size), :] for a in range(3)], axis=1
    )
    return jnp.dot(left, weight[...], preferred_element_type=F32)


def conv_t_rows(win, weight, start, size, cols, chans):
    total = None
    for a in range(3):
        left = win[pl.ds(pl.multiple_of(start + (2 - a) * cols, cols), size), :]
        for b in range(3):
            tap = (a * 3 + b) * chans
            part = lax.dot_general(
                left[:, b * chans : (b + 1) * chans],
                weight[tap : tap + chans, :],
                (((1,), (1,)), ((), ())),
                preferred_element_type=F32,
            )
            total = part if total is None else total + part
    return total


def bit_order(order):
    bits = [b for b in order[1:]]
    return bits


def slot_static(j, bits):
    s = 0
    for b in bits:
        s = s * 2 + ((j >> b) & 1)
    return s


def slot_dynamic(me, bits):
    s = jnp.int32(0)
    for b in bits:
        s = s * 2 + ((me >> b) & 1)
    return s


def store_terms(tap, value, keep, send, me, n, order, scale):
    rows = value.shape[0] // n
    value = value * scale
    bits = bit_order(order)
    mine = slot_dynamic(me, bits)
    flip = ((me >> order[0]) & 1) == 1
    for j in range(n):
        if (j >> order[0]) & 1:
            continue
        other = j ^ (1 << order[0])
        low = value[j * rows : (j + 1) * rows]
        high = value[other * rows : (other + 1) * rows]
        slot = slot_static(j, bits) ^ mine
        keep[slot, tap] = jnp.where(flip, high, low)
        send[slot, tap] = jnp.where(flip, low, high).astype(BF16)


def transposed_dot(left, right):
    return lax.dot_general(left, right, (((0,), (0,)), ((), ())), preferred_element_type=F32)


def rows_of(ref, first, count, cols):
    return ref[first * cols : (first + count) * cols, :]


def pair(ref, one, two, cols):
    return jnp.concatenate([rows_of(ref, one, 1, cols), rows_of(ref, two, 1, cols)], axis=0)


def pre_of_pair(xs, w, one, two, cols):
    left = [pair(xs, one + 1 + a, two + 1 + a, cols) for a in range(3)]
    return jnp.dot(jnp.concatenate(left, axis=1), w[...], preferred_element_type=F32)


def grad_of_pair(cs, w, one, two, cols):
    total = None
    for a in range(3):
        left = pair(cs, one + 3 - a, two + 3 - a, cols)
        chans = left.shape[1] // 3
        for b in range(3):
            tap = (a * 3 + b) * chans
            part = lax.dot_general(
                left[:, b * chans : (b + 1) * chans],
                w[tap : tap + chans, :],
                (((1,), (1,)), ((), ())),
                preferred_element_type=F32,
            )
            total = part if total is None else total + part
    return total


def derivative(pre, sigma):
    return sigma * (1.0 + pre * (1.0 - sigma))


def inner_kernel(f_hbm, c_hbm, w_hbm, w_one, xs, cs, hid, slope, acc, f, c, w_two, sems):
    rows, cols, chans = f.shape
    loads = []
    for slot, (source, target) in enumerate(((f_hbm, f), (c_hbm, c), (w_hbm, w_two))):
        piece = target.shape[0] // PIECES
        loads.append([
            pltpu.make_async_copy(
                source.at[pl.ds(j * piece, piece)],
                target.at[pl.ds(j * piece, piece)],
                sems.at[slot * PIECES + j],
            )
            for j in range(PIECES)
        ])
    for group in loads:
        for load in group:
            load.start()
    for dst, field, group, sign in ((xs, f, loads[0], 1), (cs, c, loads[1], -1)):
        piece = rows // PIECES
        for j, load in enumerate(group):
            load.wait()
            fill(dst, 2 + j * piece, piece, field, j * piece, sign)
    for load in loads[2]:
        load.wait()
    half = (rows - 2) // 2
    size = half * cols

    for k in range(2):
        start = (2 + k * half) * cols
        here = pl.ds(pl.multiple_of(start, cols), size)
        pre = conv_rows(xs, w_one, start, size, cols)
        sigma = jax.nn.sigmoid(pre)
        hid[here, :] = (pre * sigma).astype(BF16)
        grad = conv_t_rows(cs, w_two, start, size, cols, chans)
        slope[here, :] = (grad * derivative(pre, sigma)).astype(BF16)
    left = rows_of(hid, 2, rows - 2, cols)
    for a in range(3):
        acc[a] = transposed_dot(left, rows_of(cs, 4 - a, rows - 2, cols))


def edge_kernel(n, order, scale, me_ref, inside, across, w, xs_in, cs_in, hid_in, acc,
                xs, cs, hid, fac, keep, send):
    cols, chans = inside.shape[1:]
    rows = xs.shape[0] // cols - 4
    me = me_ref[0]
    odd = (me & 1) == 1
    for k in range(2):
        for dst, part, sign in ((xs, k, 1), (cs, 2 + k, -1)):
            one, two = inside[part], across[part]
            above, below = jnp.where(odd, one, two), jnp.where(odd, two, one)
            put_windows(dst, k, jnp.where(me == 0, 0.0, above).astype(BF16), sign)
            put_windows(dst, rows + 2 + k, jnp.where(me == n - 1, 0.0, below).astype(BF16), sign)
    pre = pre_of_pair(xs, w, 0, rows - 1, cols)
    sigma = jax.nn.sigmoid(pre)
    hidden = (pre * sigma).astype(BF16)
    hid[cols : 2 * cols, :] = hidden[:cols]
    hid[rows * cols : (rows + 1) * cols, :] = hidden[cols:]
    fac[...] = derivative(pre, sigma)
    left = pair(hid, 1, rows, cols)

    def part(a, carry):
        two = [
            cs[pl.ds(pl.multiple_of((first - a) * cols, cols), cols), :] for first in (3, rows + 2)
        ]
        out = acc[a] + transposed_dot(left, jnp.concatenate(two, axis=0))
        for b in range(3):
            store_terms(
                a * 3 + b, out[:, b * chans : (b + 1) * chans], keep, send, me, n, order, scale
            )
        return carry

    lax.fori_loop(0, 3, part, 0)


def terms_kernel(n, order, scale, me_ref, xs, cs, fac, w, slope_in, slope, keep, send):
    chans = slope.shape[1]
    cols = fac.shape[0] // 2
    rows = xs.shape[0] // cols - 4
    value = (grad_of_pair(cs, w, 0, rows - 1, cols) * fac[...]).astype(BF16)
    slope[cols : 2 * cols, :] = value[:cols]
    slope[rows * cols : (rows + 1) * cols, :] = value[cols:]
    right = rows_of(slope, 1, rows, cols)
    for a in range(3):
        out = transposed_dot(rows_of(xs, 1 + a, rows, cols), right)
        for b in range(3):
            store_terms(
                a * 3 + b, out[b * chans : (b + 1) * chans], keep, send, me_ref[0], n, order, scale
            )


def sides_kernel(n, cols, me_ref, xs, cs, w_one, w_two, hid_in, slope_in, hid, slope):
    rows = xs.shape[0] // cols - 4
    pre = pre_of_pair(xs, w_one, -1, rows, cols)
    grad = grad_of_pair(cs, w_two, -1, rows, cols)
    sigma = jax.nn.sigmoid(pre)
    hidden = pre * sigma
    value = grad * derivative(pre, sigma)
    for side, outside in ((0, me_ref[0] == 0), (1, me_ref[0] == n - 1)):
        here = slice(side * cols, (side + 1) * cols)
        there = slice(side * (rows + 1) * cols, (side * (rows + 1) + 1) * cols)
        hid[there, :] = jnp.where(outside, 0.0, hidden[here]).astype(BF16)
        slope[there, :] = jnp.where(outside, 0.0, value[here]).astype(BF16)


def widen_rows(hs, ss, hid, slope, first, count, cols):
    def step(k, carry):
        row = pl.ds(pl.multiple_of((first + k) * cols, cols), cols)
        put_windows(hs, k, hid[row, :], 1)
        put_windows(ss, k, slope[row, :], -1)
        return carry

    lax.fori_loop(0, count, step, 0)


def ready_kernel(first, cols, hid, slope, hs, ss):
    widen_rows(hs, ss, hid, slope, first, hs.shape[0] // cols, cols)


def outputs_kernel(first, ready, *refs):
    if ready:
        hs, ss, xs, cs, w_two, w_one = refs[:6]
        block_out, input_grad, f_done, c_done, sems = refs[-5:]
        count, cols, chans = f_done.shape
    else:
        hid, slope, xs, cs, w_two, w_one = refs[:6]
        block_out, input_grad, hs, ss, f_done, c_done, sems = refs[-7:]
        count, cols, chans = f_done.shape
        widen_rows(hs, ss, hid, slope, first, count + 2, cols)
    here = pl.ds(first, count)
    own = slice((first + 2) * cols, (first + 2 + count) * cols)
    shape = (count, cols, chans)
    total = xs[own, chans : 2 * chans].astype(F32) + conv_rows(hs, w_two, 0, count * cols, cols)
    f_done[...] = total.astype(BF16).reshape(shape)
    store_f = pltpu.make_async_copy(f_done, block_out.at[here], sems.at[0])
    store_f.start()
    grad = conv_t_rows(ss, w_one, 0, count * cols, cols, chans)
    total = cs[own, chans : 2 * chans].astype(F32) + grad
    c_done[...] = total.astype(BF16).reshape(shape)
    store_c = pltpu.make_async_copy(c_done, input_grad.at[here], sems.at[1])
    store_c.start()
    store_f.wait()
    store_c.wait()


def halve(keep, send, order, n):
    for bit in order:
        pairs = [(i, i ^ (1 << bit)) for i in range(n)]
        got = lax.ppermute(send, "tile", pairs)
        total = keep + got.astype(F32)
        half = total.shape[0] // 2
        if half:
            keep, send = total[:half], total[half:].astype(BF16)
        else:
            return jnp.swapaxes(total[0], 0, 1)


def layer(features, cotangent, weight_one, weight_two):
    _, rows, cols, chans = features.shape
    n = lax.axis_size("tile")
    scale = float(rows * n * cols) ** (-0.5)
    me = lax.axis_index("tile").astype(jnp.int32).reshape(1)
    f, c = features[0], cotangent[0]
    taps = weight_one.shape[1]
    w_one = jnp.swapaxes(weight_one, 0, 1).reshape(taps * chans, chans)
    w_two = jnp.swapaxes(weight_two, 0, 1).reshape(taps * chans, chans)

    bits = n.bit_length() - 1
    order_two = list(range(bits))
    order_one = [0, 2, 1] + list(range(3, bits)) if bits > 2 else order_two
    size, ext, wide = rows * cols, (rows + 2) * cols, 3 * chans
    flops = 2 * 9 * size * chans * chans
    smem = pl.BlockSpec(memory_space=pltpu.SMEM)

    hbm = pl.BlockSpec(memory_space=pltpu.HBM)

    def call(kernel, args, outs, scratch=(), work=flops, place=False, aliases={}, raw=0):
        specs = ([smem] if place else []) + [hbm] * raw + [WHOLE] * (len(args) - raw)
        return pl.pallas_call(
            kernel,
            out_shape=outs,
            in_specs=specs,
            out_specs=tuple(WHOLE for _ in outs),
            scratch_shapes=list(scratch),
            input_output_aliases=aliases,
            compiler_params=pltpu.CompilerParams(vmem_limit_bytes=LIMIT),
            cost_estimate=pl.CostEstimate(flops=work, bytes_accessed=4 << 20, transcendentals=0),
        )(*(((me,) if place else ()) + tuple(args)))

    inside, across = pack(me, f, c)
    across = lax.ppermute(across, ("groups", "tile"), across_pairs(lax.axis_size("groups"), n))
    inside = lax.ppermute(inside, "tile", [(i, i ^ 1) for i in range(n)])

    windows = struct((size + 4 * cols, wide), BF16)
    field = struct((ext, chans), BF16)
    kept = struct((n // 2, taps, chans // n, chans), F32)
    sent = struct((n // 2, taps, chans // n, chans), BF16)
    band = pltpu.VMEM((rows, cols, chans), BF16)
    xs, cs, hid, slope, acc = call(
        inner_kernel,
        (in_hbm(f), in_hbm(c), in_hbm(w_two), w_one),
        (windows, windows, field, field, struct((3, chans, wide), F32)),
        [band, band, pltpu.VMEM(w_two.shape, BF16), pltpu.SemaphoreType.DMA((3 * PIECES,))],
        work=3 * flops,
        raw=3,
    )
    xs, cs, hid, fac, keep_two, send_two = call(
        functools.partial(edge_kernel, n, order_two, scale),
        (inside, across, w_one, xs, cs, hid, acc),
        (windows, windows, field, struct((2 * cols, chans), F32), kept, sent),
        place=True,
        aliases={4: 0, 5: 1, 6: 2},
    )
    slope, keep_one, send_one = call(
        functools.partial(terms_kernel, n, order_one, scale),
        (xs, cs, fac, w_two, slope),
        (field, kept, sent),
        place=True,
        aliases={5: 0},
    )
    hid, slope = call(
        functools.partial(sides_kernel, n, cols),
        (xs, cs, w_one, w_two, hid, slope),
        (field, field),
        place=True,
        aliases={5: 0, 6: 1},
    )
    shares = [rows * share // sum(SHARES) for share in SHARES]
    shares[-1] = rows - sum(shares[:-1])
    outs, first = (), 0
    for part, count in enumerate(shares):
        ready = part > 0
        sources, scratch = (hid, slope), [pltpu.VMEM(((count + 2) * cols, wide), BF16)] * 2
        if ready:
            whole = struct(((count + 2) * cols, wide), BF16)
            sources, scratch = call(
                functools.partial(ready_kernel, first, cols),
                (hid, slope),
                (whole, whole),
                work=1 << 20,
            ), []
        outs = pl.pallas_call(
            functools.partial(outputs_kernel, first, ready),
            out_shape=(struct(f.shape, BF16), struct(c.shape, BF16)),
            in_specs=[WHOLE] * 6 + [hbm] * len(outs),
            out_specs=(hbm, hbm),
            scratch_shapes=scratch
            + [pltpu.VMEM((count, cols, chans), BF16)] * 2
            + [pltpu.SemaphoreType.DMA((2,))],
            input_output_aliases={6: 0, 7: 1} if outs else {},
            compiler_params=pltpu.CompilerParams(vmem_limit_bytes=LIMIT),
            cost_estimate=pl.CostEstimate(
                flops=2 * flops * count // rows, bytes_accessed=4 << 20, transcendentals=0
            ),
        )(*sources, xs, cs, w_two, w_one, *outs)
        first += count
    block_out, input_grad = outs
    grad_two = halve(keep_two, send_two, order_two, n)
    grad_one = halve(keep_one, send_one, order_one, n)
    return (block_out[None], input_grad[None], grad_one, grad_two)


def solution(mesh):
    in_specs = (P("groups", "tile", None, None), P("groups", "tile", None, None), P(), P())
    out_specs = (
        P("groups", "tile", None, None),
        P("groups", "tile", None, None),
        P("tile", "groups", None),
        P("tile", "groups", None),
    )
    return jax.shard_map(layer, mesh=mesh, in_specs=in_specs, out_specs=out_specs, check_vma=False)
```

```python
import functools

import jax
import jax.numpy as jnp
from jax import lax
from jax.experimental import pallas as pl
from jax.experimental.pallas import tpu as pltpu
from jax.sharding import PartitionSpec as P


F32 = jnp.float32
BF16 = jnp.bfloat16
WHOLE = pl.BlockSpec(memory_space=pltpu.VMEM)
LIMIT = 20 << 20
SHARES = (6, 6)
PIECES = 2


def struct(shape, dtype):
    return jax.ShapeDtypeStruct(shape, dtype)


def pack_kernel(me_ref, f, c, inside, across, sems):
    rows = f.shape[0]
    odd = (me_ref[0] & 1) == 1
    low, high = jnp.where(odd, 0, rows - 2), jnp.where(odd, rows - 2, 0)
    copies = []
    for out, row in ((across, high), (inside, low)):
        for k, field in enumerate((f, c)):
            copies.append(
                pltpu.make_async_copy(
                    field.at[pl.ds(row, 2)], out.at[pl.ds(2 * k, 2)], sems.at[len(copies)]
                )
            )
    for copy in copies:
        copy.start()
    for copy in copies:
        copy.wait()


def across_pairs(groups, n):
    pairs = []
    for group in range(groups):
        base = group * n
        pairs += [(base + i, base + i + 1) for i in range(1, n - 1, 2)]
        pairs += [(base + i + 1, base + i) for i in range(1, n - 1, 2)]
        twin = (group ^ 1) * n if groups % 2 == 0 else base
        pairs += [(base, twin), (base + n - 1, twin + n - 1)]
    return pairs


def in_hbm(array):
    return pltpu.with_memory_space_constraint(array, pltpu.HBM)


def pack(me, features, cotangent):
    out = struct((4,) + features.shape[1:], BF16)
    hbm = pl.BlockSpec(memory_space=pltpu.HBM)
    return pl.pallas_call(
        pack_kernel,
        out_shape=(out,) * 2,
        in_specs=[pl.BlockSpec(memory_space=pltpu.SMEM), hbm, hbm],
        out_specs=(WHOLE,) * 2,
        scratch_shapes=[pltpu.SemaphoreType.DMA((4,))],
        compiler_params=pltpu.CompilerParams(vmem_limit_bytes=8 << 20),
    )(me, in_hbm(features), in_hbm(cotangent))


def put_windows(dst, row, value, sign):
    cols, chans = value.shape
    zero = jnp.zeros((1, chans), value.dtype)
    before = jnp.concatenate([zero, value[: cols - 1]], axis=0)
    after = jnp.concatenate([value[1:], zero], axis=0)
    here = pl.ds(pl.multiple_of(row * cols, cols), cols)
    low, high = (before, after) if sign > 0 else (after, before)
    dst[here, 0:chans] = low
    dst[here, chans : 2 * chans] = value
    dst[here, 2 * chans : 3 * chans] = high


def fill(dst, base, count, source, first, sign):
    def step(k, carry):
        put_windows(dst, base + k, source[first + k], sign)
        return carry

    lax.fori_loop(0, count, step, 0)


def conv_rows(win, weight, start, size, cols):
    left = jnp.concatenate(
        [win[pl.ds(pl.multiple_of(start + a * cols, cols), size), :] for a in range(3)], axis=1
    )
    return jnp.dot(left, weight[...], preferred_element_type=F32)


def conv_t_rows(win, weight, start, size, cols, chans):
    total = None
    for a in range(3):
        left = win[pl.ds(pl.multiple_of(start + (2 - a) * cols, cols), size), :]
        for b in range(3):
            tap = (a * 3 + b) * chans
            part = lax.dot_general(
                left[:, b * chans : (b + 1) * chans],
                weight[tap : tap + chans, :],
                (((1,), (1,)), ((), ())),
                preferred_element_type=F32,
            )
            total = part if total is None else total + part
    return total


def bit_order(order):
    bits = [b for b in order[1:]]
    return bits


def slot_static(j, bits):
    s = 0
    for b in bits:
        s = s * 2 + ((j >> b) & 1)
    return s


def slot_dynamic(me, bits):
    s = jnp.int32(0)
    for b in bits:
        s = s * 2 + ((me >> b) & 1)
    return s


def store_terms(tap, value, keep, send, me, n, order, scale):
    rows = value.shape[0] // n
    value = value * scale
    bits = bit_order(order)
    mine = slot_dynamic(me, bits)
    flip = ((me >> order[0]) & 1) == 1
    for j in range(n):
        if (j >> order[0]) & 1:
            continue
        other = j ^ (1 << order[0])
        low = value[j * rows : (j + 1) * rows]
        high = value[other * rows : (other + 1) * rows]
        slot = slot_static(j, bits) ^ mine
        keep[slot, tap] = jnp.where(flip, high, low)
        send[slot, tap] = jnp.where(flip, low, high).astype(BF16)


def transposed_dot(left, right):
    return lax.dot_general(left, right, (((0,), (0,)), ((), ())), preferred_element_type=F32)


def rows_of(ref, first, count, cols):
    return ref[first * cols : (first + count) * cols, :]


def pair(ref, one, two, cols):
    return jnp.concatenate([rows_of(ref, one, 1, cols), rows_of(ref, two, 1, cols)], axis=0)


def pre_of_pair(xs, w, one, two, cols):
    left = [pair(xs, one + 1 + a, two + 1 + a, cols) for a in range(3)]
    return jnp.dot(jnp.concatenate(left, axis=1), w[...], preferred_element_type=F32)


def grad_of_pair(cs, w, one, two, cols):
    total = None
    for a in range(3):
        left = pair(cs, one + 3 - a, two + 3 - a, cols)
        chans = left.shape[1] // 3
        for b in range(3):
            tap = (a * 3 + b) * chans
            part = lax.dot_general(
                left[:, b * chans : (b + 1) * chans],
                w[tap : tap + chans, :],
                (((1,), (1,)), ((), ())),
                preferred_element_type=F32,
            )
            total = part if total is None else total + part
    return total


def derivative(pre, sigma):
    return sigma * (1.0 + pre * (1.0 - sigma))


def inner_kernel(f_hbm, c_hbm, w_hbm, w_one, xs, cs, hid, slope, acc, f, c, w_two, sems):
    rows, cols, chans = f.shape
    loads = []
    for slot, (source, target) in enumerate(((f_hbm, f), (c_hbm, c), (w_hbm, w_two))):
        piece = target.shape[0] // PIECES
        loads.append([
            pltpu.make_async_copy(
                source.at[pl.ds(j * piece, piece)],
                target.at[pl.ds(j * piece, piece)],
                sems.at[slot * PIECES + j],
            )
            for j in range(PIECES)
        ])
    for group in loads:
        for load in group:
            load.start()
    for dst, field, group, sign in ((xs, f, loads[0], 1), (cs, c, loads[1], -1)):
        piece = rows // PIECES
        for j, load in enumerate(group):
            load.wait()
            fill(dst, 2 + j * piece, piece, field, j * piece, sign)
    for load in loads[2]:
        load.wait()
    half = (rows - 2) // 2
    size = half * cols

    for k in range(2):
        start = (2 + k * half) * cols
        here = pl.ds(pl.multiple_of(start, cols), size)
        pre = conv_rows(xs, w_one, start, size, cols)
        sigma = jax.nn.sigmoid(pre)
        hid[here, :] = (pre * sigma).astype(BF16)
        grad = conv_t_rows(cs, w_two, start, size, cols, chans)
        slope[here, :] = (grad * derivative(pre, sigma)).astype(BF16)
    left = rows_of(hid, 2, rows - 2, cols)
    for a in range(3):
        acc[a] = transposed_dot(left, rows_of(cs, 4 - a, rows - 2, cols))


def edge_kernel(n, order, scale, me_ref, inside, across, w, xs_in, cs_in, hid_in, acc,
                xs, cs, hid, fac, keep, send):
    cols, chans = inside.shape[1:]
    rows = xs.shape[0] // cols - 4
    me = me_ref[0]
    odd = (me & 1) == 1
    for k in range(2):
        for dst, part, sign in ((xs, k, 1), (cs, 2 + k, -1)):
            one, two = inside[part], across[part]
            above, below = jnp.where(odd, one, two), jnp.where(odd, two, one)
            put_windows(dst, k, jnp.where(me == 0, 0.0, above).astype(BF16), sign)
            put_windows(dst, rows + 2 + k, jnp.where(me == n - 1, 0.0, below).astype(BF16), sign)
    pre = pre_of_pair(xs, w, 0, rows - 1, cols)
    sigma = jax.nn.sigmoid(pre)
    hidden = (pre * sigma).astype(BF16)
    hid[cols : 2 * cols, :] = hidden[:cols]
    hid[rows * cols : (rows + 1) * cols, :] = hidden[cols:]
    fac[...] = derivative(pre, sigma)
    left = pair(hid, 1, rows, cols)

    def part(a, carry):
        two = [
            cs[pl.ds(pl.multiple_of((first - a) * cols, cols), cols), :] for first in (3, rows + 2)
        ]
        out = acc[a] + transposed_dot(left, jnp.concatenate(two, axis=0))
        for b in range(3):
            store_terms(
                a * 3 + b, out[:, b * chans : (b + 1) * chans], keep, send, me, n, order, scale
            )
        return carry

    lax.fori_loop(0, 3, part, 0)


def terms_kernel(n, order, scale, me_ref, xs, cs, fac, w, slope_in, slope, keep, send):
    chans = slope.shape[1]
    cols = fac.shape[0] // 2
    rows = xs.shape[0] // cols - 4
    value = (grad_of_pair(cs, w, 0, rows - 1, cols) * fac[...]).astype(BF16)
    slope[cols : 2 * cols, :] = value[:cols]
    slope[rows * cols : (rows + 1) * cols, :] = value[cols:]
    right = rows_of(slope, 1, rows, cols)
    for a in range(3):
        out = transposed_dot(rows_of(xs, 1 + a, rows, cols), right)
        for b in range(3):
            store_terms(
                a * 3 + b, out[b * chans : (b + 1) * chans], keep, send, me_ref[0], n, order, scale
            )


def sides_kernel(n, cols, me_ref, xs, cs, w_one, w_two, hid_in, slope_in, hid, slope):
    rows = xs.shape[0] // cols - 4
    pre = pre_of_pair(xs, w_one, -1, rows, cols)
    grad = grad_of_pair(cs, w_two, -1, rows, cols)
    sigma = jax.nn.sigmoid(pre)
    hidden = pre * sigma
    value = grad * derivative(pre, sigma)
    for side, outside in ((0, me_ref[0] == 0), (1, me_ref[0] == n - 1)):
        here = slice(side * cols, (side + 1) * cols)
        there = slice(side * (rows + 1) * cols, (side * (rows + 1) + 1) * cols)
        hid[there, :] = jnp.where(outside, 0.0, hidden[here]).astype(BF16)
        slope[there, :] = jnp.where(outside, 0.0, value[here]).astype(BF16)


def widen_rows(hs, ss, hid, slope, first, count, cols):
    def step(k, carry):
        row = pl.ds(pl.multiple_of((first + k) * cols, cols), cols)
        put_windows(hs, k, hid[row, :], 1)
        put_windows(ss, k, slope[row, :], -1)
        return carry

    lax.fori_loop(0, count, step, 0)


def ready_kernel(first, cols, hid, slope, hs, ss):
    widen_rows(hs, ss, hid, slope, first, hs.shape[0] // cols, cols)


def gate_kernel(source, out):
    out[...] = source[: out.shape[0], : out.shape[1]].astype(F32)


def outputs_kernel(first, ready, *refs):
    if ready:
        hs, ss, xs, cs, w_two, w_one = refs[:6]
        block_out, input_grad, f_done, c_done, sems = refs[-5:]
        count, cols, chans = f_done.shape
    else:
        hid, slope, xs, cs, w_two, w_one = refs[:6]
        block_out, input_grad, hs, ss, f_done, c_done, sems = refs[-7:]
        count, cols, chans = f_done.shape
        widen_rows(hs, ss, hid, slope, first, count + 2, cols)
    here = pl.ds(first, count)
    own = slice((first + 2) * cols, (first + 2 + count) * cols)
    shape = (count, cols, chans)
    total = xs[own, chans : 2 * chans].astype(F32) + conv_rows(hs, w_two, 0, count * cols, cols)
    f_done[...] = total.astype(BF16).reshape(shape)
    store_f = pltpu.make_async_copy(f_done, block_out.at[here], sems.at[0])
    store_f.start()
    grad = conv_t_rows(ss, w_one, 0, count * cols, cols, chans)
    total = cs[own, chans : 2 * chans].astype(F32) + grad
    c_done[...] = total.astype(BF16).reshape(shape)
    store_c = pltpu.make_async_copy(c_done, input_grad.at[here], sems.at[1])
    store_c.start()
    store_f.wait()
    store_c.wait()


def halve(keep, send, order, n):
    for bit in order:
        pairs = [(i, i ^ (1 << bit)) for i in range(n)]
        got = lax.ppermute(send, "tile", pairs)
        half = keep.shape[0] // 2
        if not half:
            return keep[0], got[0]
        total = keep + got.astype(F32)
        keep, send = total[:half], total[half:].astype(BF16)


def final_kernel(kept_one, got_one, kept_two, got_two, grad_one, grad_two):
    grad_one[...] = kept_one[...] + got_one[...].astype(F32)
    grad_two[...] = kept_two[...] + got_two[...].astype(F32)


def layer(features, cotangent, weight_one, weight_two):
    _, rows, cols, chans = features.shape
    n = lax.axis_size("tile")
    scale = float(rows * n * cols) ** (-0.5)
    me = lax.axis_index("tile").astype(jnp.int32).reshape(1)
    f, c = features[0], cotangent[0]
    taps = weight_one.shape[1]
    w_one = jnp.swapaxes(weight_one, 0, 1).reshape(taps * chans, chans)
    w_two = jnp.swapaxes(weight_two, 0, 1).reshape(taps * chans, chans)

    bits = n.bit_length() - 1
    order_two = list(range(bits))
    order_one = [0, 2, 1] + list(range(3, bits)) if bits > 2 else order_two
    size, ext, wide = rows * cols, (rows + 2) * cols, 3 * chans
    flops = 2 * 9 * size * chans * chans
    smem = pl.BlockSpec(memory_space=pltpu.SMEM)

    hbm = pl.BlockSpec(memory_space=pltpu.HBM)

    def call(kernel, args, outs, scratch=(), work=flops, place=False, aliases={}, raw=0):
        specs = ([smem] if place else []) + [hbm] * raw + [WHOLE] * (len(args) - raw)
        return pl.pallas_call(
            kernel,
            out_shape=outs,
            in_specs=specs,
            out_specs=tuple(WHOLE for _ in outs),
            scratch_shapes=list(scratch),
            input_output_aliases=aliases,
            compiler_params=pltpu.CompilerParams(vmem_limit_bytes=LIMIT),
            cost_estimate=pl.CostEstimate(flops=work, bytes_accessed=4 << 20, transcendentals=0),
        )(*(((me,) if place else ()) + tuple(args)))

    inside, across = pack(me, f, c)
    across = lax.ppermute(across, ("groups", "tile"), across_pairs(lax.axis_size("groups"), n))
    inside = lax.ppermute(inside, "tile", [(i, i ^ 1) for i in range(n)])

    windows = struct((size + 4 * cols, wide), BF16)
    field = struct((ext, chans), BF16)
    kept = struct((n // 2, taps, chans // n, chans), F32)
    sent = struct((n // 2, taps, chans // n, chans), BF16)
    band = pltpu.VMEM((rows, cols, chans), BF16)
    xs, cs, hid, slope, acc = call(
        inner_kernel,
        (in_hbm(f), in_hbm(c), in_hbm(w_two), w_one),
        (windows, windows, field, field, struct((3, chans, wide), F32)),
        [band, band, pltpu.VMEM(w_two.shape, BF16), pltpu.SemaphoreType.DMA((3 * PIECES,))],
        work=3 * flops,
        raw=3,
    )
    xs, cs, hid, fac, keep_two, send_two = call(
        functools.partial(edge_kernel, n, order_two, scale),
        (inside, across, w_one, xs, cs, hid, acc),
        (windows, windows, field, struct((2 * cols, chans), F32), kept, sent),
        place=True,
        aliases={4: 0, 5: 1, 6: 2},
    )
    slope, keep_one, send_one = call(
        functools.partial(terms_kernel, n, order_one, scale),
        (xs, cs, fac, w_two, slope),
        (field, kept, sent),
        place=True,
        aliases={5: 0},
    )
    hid, slope = call(
        functools.partial(sides_kernel, n, cols),
        (xs, cs, w_one, w_two, hid, slope),
        (field, field),
        place=True,
        aliases={5: 0, 6: 1},
    )
    shares = [rows * share // sum(SHARES) for share in SHARES]
    shares[-1] = rows - sum(shares[:-1])
    outs, first = (), 0
    for part, count in enumerate(shares):
        ready = part > 0
        sources, scratch = (hid, slope), [pltpu.VMEM(((count + 2) * cols, wide), BF16)] * 2
        if ready:
            whole = struct(((count + 2) * cols, wide), BF16)
            sources, scratch = call(
                functools.partial(ready_kernel, first, cols),
                (hid, slope),
                (whole, whole),
                work=1 << 20,
            ), []
        gates = ()
        if ready:
            gates = call(gate_kernel, (hid,), (struct((8, 128), F32),), work=1 << 10)
        outs = pl.pallas_call(
            functools.partial(outputs_kernel, first, ready),
            out_shape=(struct(f.shape, BF16), struct(c.shape, BF16)),
            in_specs=[WHOLE] * 6 + [hbm] * len(outs) + [WHOLE] * len(gates),
            out_specs=(hbm, hbm),
            scratch_shapes=scratch
            + [pltpu.VMEM((count, cols, chans), BF16)] * 2
            + [pltpu.SemaphoreType.DMA((2,))],
            input_output_aliases={6: 0, 7: 1} if outs else {},
            compiler_params=pltpu.CompilerParams(vmem_limit_bytes=LIMIT),
            cost_estimate=pl.CostEstimate(
                flops=2 * flops * count // rows, bytes_accessed=4 << 20, transcendentals=0
            ),
        )(*sources, xs, cs, w_two, w_one, *outs, *gates)
        first += count
    block_out, input_grad = outs
    last_two = halve(keep_two, send_two, order_two, n)
    last_one = halve(keep_one, send_one, order_one, n)
    slab = struct(last_one[0].shape, F32)
    grads = call(final_kernel, last_one + last_two, (slab, slab), work=1 << 20)
    grad_one, grad_two = (jnp.swapaxes(grad, 0, 1) for grad in grads)
    return (block_out[None], input_grad[None], grad_one, grad_two)


def solution(mesh):
    in_specs = (P("groups", "tile", None, None), P("groups", "tile", None, None), P(), P())
    out_specs = (
        P("groups", "tile", None, None),
        P("groups", "tile", None, None),
        P("tile", "groups", None),
        P("tile", "groups", None),
    )
    return jax.shard_map(layer, mesh=mesh, in_specs=in_specs, out_specs=out_specs, check_vma=False)
```
